512 devices in a mesh: stream: 32 (over x, z), span: 16 (over y, core).
Axes of the slice: x: 4, y: 8, z: 8, core: 2. Of those that a mesh axis runs over, the one named last changes fastest.
Arguments:
- rhs: float32 [32, 16, 2, 320, 128], P('stream', 'span'), may hold values from -6 to 6
- inv_blocks: bfloat16 [32, 16, 2, 320, 320], P('stream', 'span')
- coupling: bfloat16 [6, 320, 320], replicated, may hold values from -0.109375 to 0.109375
- trace_ops: bfloat16 [4, 80, 320], replicated, may hold values from -0.3125 to 0.3125
- lift_ops: bfloat16 [4, 320, 80], replicated
- order: int32 [32, 16, 2], P('stream', 'span'), may hold values from 0 to 1, each once within a row
- counts: int32 [32, 16], P('stream', 'span'), may hold values from 1 to 2, as said below
- neighbours: int32 [32, 16, 2, 2], P('stream', 'span'), may hold values from 0 to 2, as said below
- face_ids: int32 [32, 16, 2, 2], P('stream', 'span'), may hold values from 0 to 5
Outputs:
- solution: float32 [32, 16, 2, 320, 128], P('stream', 'span')
The draws below stay inside these ranges and needn't reach their ends.
Inputs may be any that keep to these rules, and one draw needn't show every extreme that they name: order[i, j] lists each of the 2 slots of line (i, j) once. `counts`: some line holds 2 live elements and some line 1. `neighbours`: a slot of the same line other than the element's own, or 2 where the face has no in-line neighbour.
All inputs are finite; a program needn't handle non-finite values.
Results may differ from the reference program's by a relative error of at most 0.00075.
Values sent between devices are 32-bit elements; how exact they have to be, the bound alone decides.
A program may use at most 64 MiB of HBM per device.

```python
import math
from functools import partial
import jax
import jax.numpy as jnp
from jax import lax

B = 320
TF = 80
E = 2
NL = 2
FT = 6
R = 128
SWEEPS = 2
LINES_X = 32
LINES_Z = 16


def draw_inv_blocks(key, part):
    noise = jax.random.normal(key, (LINES_X, LINES_Z, E, B, B), jnp.float32)
    identity_block = jnp.eye(B, dtype=jnp.float32)
    return (0.7 * (identity_block + 0.4 * noise / math.sqrt(B))).astype(jnp.bfloat16)


def draw_lift_ops(key, part):
    noise = jax.random.normal(key, (4, B, TF), jnp.float32)
    face_scales = jnp.array([1.3, 1.3, 0.4, 0.4], jnp.float32)
    return (noise * face_scales[:, None, None] / math.sqrt(TF)).astype(jnp.bfloat16)


def draw_counts(key, part):
    line_total = LINES_X * LINES_Z
    drops = (jax.random.randint(key, (line_total,), 0, 4) == 0).astype(jnp.int32)
    raw_counts = E - drops
    chosen = jax.random.randint(jax.random.fold_in(key, 7), (), 0, line_total)
    step_away = jax.random.randint(jax.random.fold_in(key, 9), (), 1, line_total)
    other = (chosen + step_away) % line_total
    filled = raw_counts.at[chosen].set(E).at[other].set(E - 1)
    return filled.reshape(LINES_X, LINES_Z).astype(jnp.int32)


def draw_neighbours(key, part):
    offset_key = jax.random.fold_in(key, 11)
    absent_key = jax.random.fold_in(key, 13)
    offsets = jax.random.randint(offset_key, (LINES_X, LINES_Z, E, NL), 1, E)
    slot_ids = jnp.arange(E, dtype=jnp.int32)[None, None, :, None]
    targets = (slot_ids + offsets) % E
    absent = jax.random.randint(absent_key, (LINES_X, LINES_Z, E, NL), 0, 4) == 0
    return jnp.where(absent, E, targets).astype(jnp.int32)


def touch_ends(drawn, stream_key, least, high):
    spot = [jax.random.randint(jax.random.fold_in(stream_key, axis), (), 0, length) for axis, length in enumerate(drawn.shape)]
    widest = drawn.shape.index(max(drawn.shape))
    next_to = spot[:widest] + [(spot[widest] + 1) % drawn.shape[widest]] + spot[widest + 1:]
    return drawn.at[tuple(spot)].set(least).at[tuple(next_to)].set(high)


def levels(stream_key, shape, split, smallest, top_value):
    loudness = 1.0
    for dim, shards_of in split:
        steps = jax.random.uniform(jax.random.fold_in(jax.random.fold_in(stream_key, 6), dim), (shards_of,), jnp.float32, smallest / len(split), top_value / len(split))
        loudness = loudness * jnp.repeat(jnp.exp(steps), shape[dim] // shards_of).reshape((-1,) + (1,) * (len(shape) - 1 - dim))
    return loudness


def normal_values(rng, extent, scale, limit, cuts=(), held_as=jnp.bfloat16):
    values = jax.random.normal(rng, extent, jnp.float32) * scale
    if len(cuts) > 0:
        values = levels(rng, extent, cuts, -0.22, 0.18) * values
    return jnp.clip(values, min=-limit, max=limit).astype(held_as)


def setup_inputs(seed: int = 0) -> dict:
    seeds = jax.random.split(jax.random.key(seed), 10)
    rhs = normal_values(seeds[0], (LINES_X, LINES_Z, E, B, R), 1.0, 6.0, ((0, 32), (1, 16)), jnp.float32)
    inv_blocks = draw_inv_blocks(jax.random.fold_in(seeds[9], 71), 0)
    coupling = normal_values(seeds[2], (FT, B, B), (B * 11) ** -0.5, 0.109375)
    trace_ops = normal_values(seeds[3], (4, TF, B), B ** -0.5, 0.3125)
    lift_ops = draw_lift_ops(jax.random.fold_in(seeds[9], 71), 0)
    order = jax.vmap(lambda own: jax.random.permutation(own, E))(jax.random.split(seeds[5], LINES_X * LINES_Z)).reshape((LINES_X, LINES_Z, E)).astype(jnp.int32)
    counts = draw_counts(jax.random.fold_in(seeds[9], 71), 0)
    neighbours = draw_neighbours(jax.random.fold_in(seeds[9], 71), 0)
    face_ids = touch_ends(jax.random.randint(seeds[8], (LINES_X, LINES_Z, E, NL), 0, FT), jax.random.fold_in(seeds[8], 1), 0, FT - 1).astype(jnp.int32)
    return {"rhs": rhs, "inv_blocks": inv_blocks, "coupling": coupling, "trace_ops": trace_ops, "lift_ops": lift_ops, "order": order, "counts": counts, "neighbours": neighbours, "face_ids": face_ids}


HIGH = lax.Precision.HIGHEST


def column_sweep(solution, residual, inverse, order, count, neighbours, face_ids, coupling, backward):
    slot_count = solution.shape[0]
    positions = range(slot_count - 1, -1, -1) if backward else range(slot_count)
    for position in positions:
        slot_index = order[position]
        residual_now = lax.dynamic_index_in_dim(residual, slot_index, 0, keepdims=False)
        for face_index in range(neighbours.shape[1]):
            neighbour_slot = neighbours[slot_index, face_index]
            present = neighbour_slot < slot_count
            neighbour_block = lax.dynamic_index_in_dim(solution, jnp.minimum(neighbour_slot, slot_count - 1), 0, keepdims=False)
            coupling_block = lax.dynamic_index_in_dim(coupling, face_ids[slot_index, face_index], 0, keepdims=False)
            product = jnp.dot(coupling_block, neighbour_block, precision=HIGH)
            residual_now = residual_now - jnp.where(present, product, jnp.zeros_like(product))
        inverse_block = lax.dynamic_index_in_dim(inverse, slot_index, 0, keepdims=False).astype(jnp.float32)
        live_factor = (position < count).astype(jnp.float32)
        updated = jnp.dot(inverse_block, residual_now, precision=HIGH) * live_factor
        solution = lax.dynamic_update_index_in_dim(solution, updated, slot_index, 0)
    return solution


def apply_trace(operator, values):
    return jnp.einsum('tb,...br->...tr', operator, values, precision=HIGH)


def apply_lift(operator, traces):
    return jnp.einsum('bt,...tr->...br', operator, traces, precision=HIGH)


def half_sweep(solution, backward, rhs, inv_blocks, coupling_table, traces_op, lifts, order, counts, neighbours, face_ids):
    left_traces = jnp.roll(apply_trace(traces_op[3], solution), 1, axis=1)
    right_traces = jnp.roll(apply_trace(traces_op[2], solution), -1, axis=1)
    residual_base = rhs - apply_lift(lifts[2], left_traces) - apply_lift(lifts[3], right_traces)
    zero_layer = jnp.zeros_like(left_traces[:1])
    if backward:
        previous = jnp.concatenate([zero_layer, apply_trace(traces_op[1], solution)[:-1]], axis=0)
        residual_base = residual_base - apply_lift(lifts[0], previous)
        inflow_lift = lifts[1]
        outflow_trace = traces_op[0]
    else:
        previous = jnp.concatenate([apply_trace(traces_op[0], solution)[1:], zero_layer], axis=0)
        residual_base = residual_base - apply_lift(lifts[1], previous)
        inflow_lift = lifts[0]
        outflow_trace = traces_op[1]
    line_sweep = jax.vmap(partial(column_sweep, coupling=coupling_table, backward=backward))

    def step(carried, items):
        column, base_column, inverse_column, order_column, count_column, link_column, type_column = items
        residual_column = base_column - apply_lift(inflow_lift, carried)
        updated = line_sweep(column, residual_column, inverse_column, order_column, count_column, link_column, type_column)
        return apply_trace(outflow_trace, updated), updated

    initial = jnp.zeros(left_traces.shape[1:], jnp.float32)
    _, result = lax.scan(step, initial, (solution, residual_base, inv_blocks, order, counts, neighbours, face_ids), reverse=backward)
    return result


def reference(rhs, inv_blocks, coupling, trace_ops, lift_ops, order, counts, neighbours, face_ids):
    coupling_table = coupling.astype(jnp.float32)
    traces_op = trace_ops.astype(jnp.float32)
    lifts = lift_ops.astype(jnp.float32)
    solution = jnp.zeros_like(rhs)
    for sweep_index in range(SWEEPS):
        solution = half_sweep(solution, False, rhs, inv_blocks, coupling_table, traces_op, lifts, order, counts, neighbours, face_ids)
        solution = half_sweep(solution, True, rhs, inv_blocks, coupling_table, traces_op, lifts, order, counts, neighbours, face_ids)
    return solution
```

```python
import functools

import jax
import jax.numpy as jnp
from jax import lax
from jax.experimental import pallas as pl
from jax.experimental.pallas import tpu as pltpu
from jax.sharding import PartitionSpec as P

MESH = pl.DeviceIdType.MESH
F32 = jnp.float32
BF16 = jnp.bfloat16
SWEEPS = 2
B = 320
TF = 80
W = 128


def split(v):
    high = v.astype(BF16)
    return high, (v - high.astype(F32)).astype(BF16)


def apply(operator, v):
    high, low = split(v)
    both = jnp.dot(operator, jnp.concatenate([high, low], axis=1), preferred_element_type=F32)
    return both[:, :W] + both[:, W:]


def nt(a, b):
    return lax.dot_general(a, b, (((1,), (1,)), ((), ())), preferred_element_type=F32)


def through(v, high_map, low_map):
    high, low = split(v)
    rows = v.shape[0]
    both = nt(jnp.concatenate([high, low], axis=0), high_map)
    return both[:rows] + both[rows:] + nt(high, low_map)


def kernel(
    NX, NZ, NS,
    order_ref, count_ref, nbr_ref, fid_ref, rhs_ref, inv_ref, coup_ref, trop_ref, lift_ref,
    out_ref,
    invs, coups, lpad, tpad, base, resid, field,
    tmsg, tmap, cmap, sstage, sbuf, lbuf, ostage, wbuf, xstage, xbuf, icur, pstage, pbuf,
    tsend, trecv, asend, arecv, bsend, brecv, xsend, xrecv, psend, precv,
):
    CH = W // NZ
    i = lax.axis_index("stream")
    j = lax.axis_index("span")
    z = lax.rem(i, NZ)
    x = lax.div(i, NZ)

    def at_z(offset):
        return lax.rem(z + (offset + NZ), NZ)

    def line_z(zz):
        return (x * NZ + zz, j)

    span_left = (i, lax.rem(j + NS - 1, NS))
    span_right = (i, lax.rem(j + 1, NS))
    x_next = (lax.rem(x + 1, NX) * NZ + z, j)
    x_prev = (lax.rem(x + NX - 1, NX) * NZ + z, j)

    barrier = pltpu.get_barrier_semaphore()
    greeted = [line_z(at_z(d)) for d in range(1, NZ)] + [x_next, x_prev, span_left, span_right]
    for device in greeted:
        pl.semaphore_signal(barrier, inc=1, device_id=device, device_id_type=MESH)

    a = order_ref[0, 0, 0]
    b = order_ref[0, 0, 1]
    a_is_0 = a == 0
    live = count_ref[0, 0] > 1
    zero_block = jnp.zeros((B, B), BF16)
    invs[0] = inv_ref[a]
    invs[1] = jnp.where(live, inv_ref[b], zero_block)
    for pos, slot in ((0, a), (1, b)):
        for m in range(2):
            present = nbr_ref[0, 0, slot, m] < 2
            coups[pos, m] = jnp.where(present, coup_ref[fid_ref[0, 0, slot, m]], zero_block)
        base[pos] = rhs_ref[slot]
        resid[pos] = rhs_ref[slot]
        field[pos] = jnp.zeros((B, W), F32)
    lpad[...] = jnp.zeros((2, B, W), BF16)
    tpad[...] = jnp.zeros((2, W, B), BF16)
    for d in range(2):
        lpad[d, :, 0:TF] = lift_ref[d]
        tpad[d, 0:TF, :] = trop_ref[1 - d]
    tmap[...] = jnp.zeros(tmap.shape, BF16)

    def coupled(pos, v):
        high, low = split(v)
        v2 = jnp.concatenate([high, low], axis=1)
        both = jnp.dot(coups[pos, 0], v2, preferred_element_type=F32) + jnp.dot(
            coups[pos, 1], v2, preferred_element_type=F32
        )
        return both[:, :W] + both[:, W:]

    lane = lax.broadcasted_iota(jnp.int32, (TF, W), 1)

    def own_map(d):
        first, second = (0, 1) if d == 0 else (1, 0)
        u1 = jnp.dot(invs[first], lpad[d], preferred_element_type=F32)
        u2 = jnp.dot(invs[second], lpad[d], preferred_element_type=F32)
        v = apply(invs[second], coupled(second, u1))
        trace = trop_ref[1 - d]
        t11 = -apply(trace, u1)
        t22 = -apply(trace, u2)
        t21 = apply(trace, v)
        first_is_0 = jnp.where(a_is_0, 1.0 - d, 0.0 + d).astype(F32)
        flag = jnp.zeros((TF, W), F32) + first_is_0
        upper = jnp.where(lane < TF, t11, jnp.where(lane < 112, pltpu.roll(t22, 32, 1), flag))
        lower = jnp.where(lane < TF, t21, pltpu.roll(t22, TF, 1))
        tmsg[d, z, 0:TF, :] = upper
        tmsg[d, z, TF : 2 * TF, :] = lower

    def unpack(d, zz):
        p = zz if d == 0 else NZ - 1 - zz
        upper = tmsg[d, zz, 0:TF, :]
        lower = tmsg[d, zz, TF : 2 * TF, :]
        flag = jnp.sum(jnp.where(lane == 120, upper, 0.0), axis=1, keepdims=True) > 0.5
        zero = jnp.zeros((TF, W), F32)
        t11 = jnp.where(lane < TF, upper, zero)
        t21 = jnp.where(lane < TF, lower, zero)
        t22 = jnp.where(
            lane < 48,
            pltpu.roll(lower, 48, 1),
            jnp.where(lane < TF, pltpu.roll(upper, 96, 1), zero),
        )
        blocks = (
            (0, 0, jnp.where(flag, t11, t22)),
            (0, W, jnp.where(flag, zero, t21)),
            (W, 0, jnp.where(flag, t21, zero)),
            (W, W, jnp.where(flag, t22, t11)),
        )
        for row, col, block in blocks:
            high, low = split(block)
            tmap[d, p, 0, row : row + TF, col : col + W] = high
            tmap[d, p, 1, row : row + TF, col : col + W] = low

    def t_copy(d, ring, k, zz):
        step = 1 if ring == 0 else -1
        return pltpu.make_async_remote_copy(
            src_ref=tmsg.at[d, zz],
            dst_ref=tmsg.at[d, zz],
            send_sem=tsend.at[d, ring, k],
            recv_sem=trecv.at[d, ring, k],
            device_id=line_z(at_z(step)),
            device_id_type=MESH,
        )

    reach = (NZ // 2, NZ - 1 - NZ // 2)
    for d in range(2):
        own_map(d)
        if d == 0:
            pl.semaphore_wait(barrier, len(greeted))
        for ring in range(2):
            if reach[ring] > 0:
                t_copy(d, ring, 0, z).start()
    for d in range(2):
        unpack(d, z)
    for k in range(1, NZ // 2 + 1):
        for d in range(2):
            for ring in range(2):
                if k > reach[ring]:
                    continue
                source = at_z(-k if ring == 0 else k)
                t_copy(d, ring, k - 1, source).wait_recv()
                if k < reach[ring]:
                    t_copy(d, ring, k, source).start()
            for ring in range(2):
                if k <= reach[ring]:
                    unpack(d, at_z(-k if ring == 0 else k))
    for d in range(2):
        for ring in range(2):
            for k in range(reach[ring]):
                t_copy(d, ring, k, at_z(-k if ring == 0 else k)).wait_send()

    for d in range(2):
        row = lax.broadcasted_iota(jnp.int32, (2 * W, 2 * W), 0)
        col = lax.broadcasted_iota(jnp.int32, (2 * W, 2 * W), 1)
        cmap[d, 0, 0] = jnp.where(row == col, 1.0, 0.0).astype(BF16)
        cmap[d, 0, 1] = jnp.zeros((2 * W, 2 * W), BF16)
        cmap[d, 1] = tmap[d, 0]

        def cumulate(p, carry, d=d):
            high, low = cmap[d, p, 0], cmap[d, p, 1]
            joined = (
                jnp.dot(tmap[d, p, 0], high, preferred_element_type=F32)
                + jnp.dot(tmap[d, p, 0], low, preferred_element_type=F32)
                + jnp.dot(tmap[d, p, 1], high, preferred_element_type=F32)
            )
            high, low = split(joined)
            cmap[d, p + 1, 0] = high
            cmap[d, p + 1, 1] = low
            return carry

        lax.fori_loop(1, NZ, cumulate, 0)

    far_first = sorted(range(1, NZ), key=lambda d: (-min(d, NZ - d), d))

    def a_copy(h, d):
        zz = at_z(d)
        return pltpu.make_async_remote_copy(
            src_ref=sstage.at[h, pl.ds(pl.multiple_of(zz * CH, CH), CH), :],
            dst_ref=sbuf.at[h, z],
            send_sem=asend.at[h, d],
            recv_sem=arecv.at[h, d],
            device_id=line_z(zz),
            device_id_type=MESH,
        )

    def b_copy(h, d):
        return pltpu.make_async_remote_copy(
            src_ref=ostage.at[h, d],
            dst_ref=wbuf.at[h, pl.ds(pl.multiple_of(z * CH, CH), CH), :],
            send_sem=bsend.at[h, d],
            recv_sem=brecv.at[h, d],
            device_id=line_z(at_z(d)),
            device_id_type=MESH,
        )

    def x_copy(h, device):
        return pltpu.make_async_remote_copy(
            src_ref=xstage.at[h],
            dst_ref=xbuf.at[h],
            send_sem=xsend.at[h],
            recv_sem=xrecv.at[h],
            device_id=device,
            device_id_type=MESH,
        )

    def p_copy(h, side, device):
        return pltpu.make_async_remote_copy(
            src_ref=pstage.at[h, side],
            dst_ref=pbuf.at[h, side],
            send_sem=psend.at[h, side],
            recv_sem=precv.at[h, side],
            device_id=device,
            device_id_type=MESH,
        )

    def half_sweep(k, d):
        h = 2 * k + d
        first, second = (0, 1) if d == 0 else (1, 0)
        x1 = apply(invs[first], resid[first] - coupled(first, field[second]))
        x2 = apply(invs[second], resid[second] - coupled(second, x1))
        s1 = apply(tpad[d], x1)
        s2 = apply(tpad[d], x2)
        sa, sb = (s1, s2) if d == 0 else (s2, s1)
        sstage[h, :, 0:W] = jnp.where(a_is_0, sa, sb).T
        sstage[h, :, W : 2 * W] = jnp.where(a_is_0, sb, sa).T
        for dist in far_first:
            a_copy(h, dist).start()
        sbuf[h, z] = sstage[h, pl.ds(pl.multiple_of(z * CH, CH), CH), :]
        for dist in far_first:
            a_copy(h, dist).wait_recv()

        v = jnp.zeros((CH, 2 * W), F32)
        for p in range(NZ):
            lbuf[p] = v
            new = sbuf[h, p if d == 0 else NZ - 1 - p]
            v = new if p == 0 else through(v, tmap[d, p, 0], tmap[d, p, 1]) + new

        xp = x if d == 0 else NX - 1 - x
        ahead, behind = (x_next, x_prev) if d == 0 else (x_prev, x_next)

        @pl.when(xp == 0)
        def _():
            icur[...] = jnp.zeros((CH, 2 * W), F32)

        @pl.when(xp > 0)
        def _():
            x_copy(h, behind).wait_recv()
            icur[...] = xbuf[h]

        inflow = icur[...]

        @pl.when(xp < NX - 1)
        def _():
            xstage[h] = v + through(inflow, cmap[d, NZ, 0], cmap[d, NZ, 1])
            x_copy(h, ahead).start()

        for dist in far_first + [0]:
            zz = at_z(dist)
            p = zz if d == 0 else NZ - 1 - zz
            piece = lbuf[p] + through(inflow, cmap[d, p, 0], cmap[d, p, 1])
            if dist:
                ostage[h, dist] = piece
                b_copy(h, dist).start()
            else:
                wbuf[h, pl.ds(pl.multiple_of(z * CH, CH), CH), :] = piece
        for dist in far_first:
            b_copy(h, dist).wait_recv()

        w0 = wbuf[h, :, 0:W].T[0:TF]
        w1 = wbuf[h, :, W : 2 * W].T[0:TF]
        wa = jnp.where(a_is_0, w0, w1)
        wb = jnp.where(a_is_0, w1, w0)
        lifted = (apply(lift_ref[d], wa), apply(lift_ref[d], wb))
        y1 = apply(invs[first], lifted[first])
        y2 = apply(invs[second], lifted[second] - coupled(second, y1))
        x1 = x1 - y1
        x2 = x2 - y2
        field[first] = x1
        field[second] = x2

        def exchange():
            xa, xb = (x1, x2) if d == 0 else (x2, x1)
            for side, trace, device in ((0, 3, span_right), (1, 2, span_left)):
                ta = apply(trop_ref[trace], xa)
                tb = apply(trop_ref[trace], xb)
                pstage[h, side, 0] = jnp.where(a_is_0, ta, tb)
                pstage[h, side, 1] = jnp.where(a_is_0, tb, ta)
                p_copy(h, side, device).start()
            rest = [base[pos] - lifted[pos] for pos in range(2)]
            p_copy(h, 0, span_right).wait_recv()
            p_copy(h, 1, span_left).wait_recv()
            for pos in range(2):
                total = rest[pos]
                for side in range(2):
                    t0 = pbuf[h, side, 0]
                    t1 = pbuf[h, side, 1]
                    mine, other = (t0, t1) if pos == 0 else (t1, t0)
                    total = total - apply(lift_ref[2 + side], jnp.where(a_is_0, mine, other))
                resid[pos] = total
            p_copy(h, 0, span_right).wait_send()
            p_copy(h, 1, span_left).wait_send()

        if d == 0:
            exchange()
        else:
            pl.when(k < SWEEPS - 1)(exchange)

        for dist in far_first:
            a_copy(h, dist).wait_send()
            b_copy(h, dist).wait_send()

        @pl.when(xp < NX - 1)
        def _():
            x_copy(h, ahead).wait_send()

    def sweep(k, carry):
        half_sweep(k, 0)
        half_sweep(k, 1)
        return carry

    lax.fori_loop(0, SWEEPS, sweep, 0)
    out_ref[0] = jnp.where(a_is_0, field[0], field[1])
    out_ref[1] = jnp.where(a_is_0, field[1], field[0])


def solution(mesh):
    lines = mesh.shape["stream"]
    NZ = {32: 8, 8: 4, 4: 2}[lines]
    NX = lines // NZ
    NS = mesh.shape["span"]
    CH = W // NZ
    H = 2 * SWEEPS

    def local(rhs, inv_blocks, coupling, trace_ops, lift_ops, order, counts, neighbours, face_ids):
        vmem = pl.BlockSpec(memory_space=pltpu.VMEM)
        smem = pl.BlockSpec(memory_space=pltpu.SMEM)
        dma = pltpu.SemaphoreType.DMA
        call = pl.pallas_call(
            functools.partial(kernel, NX, NZ, NS),
            out_shape=jax.ShapeDtypeStruct((2, B, W), F32),
            in_specs=[smem] * 4 + [vmem] * 5,
            out_specs=vmem,
            scratch_shapes=[
                pltpu.VMEM((2, B, B), BF16),
                pltpu.VMEM((2, 2, B, B), BF16),
                pltpu.VMEM((2, B, W), BF16),
                pltpu.VMEM((2, W, B), BF16),
                pltpu.VMEM((2, B, W), F32),
                pltpu.VMEM((2, B, W), F32),
                pltpu.VMEM((2, B, W), F32),
                pltpu.VMEM((2, NZ, 2 * TF, W), F32),
                pltpu.VMEM((2, NZ, 2, 2 * W, 2 * W), BF16),
                pltpu.VMEM((2, NZ + 1, 2, 2 * W, 2 * W), BF16),
                pltpu.VMEM((H, W, 2 * W), F32),
                pltpu.VMEM((H, NZ, CH, 2 * W), F32),
                pltpu.VMEM((NZ, CH, 2 * W), F32),
                pltpu.VMEM((H, NZ, CH, 2 * W), F32),
                pltpu.VMEM((H, W, 2 * W), F32),
                pltpu.VMEM((H, CH, 2 * W), F32),
                pltpu.VMEM((H, CH, 2 * W), F32),
                pltpu.VMEM((CH, 2 * W), F32),
                pltpu.VMEM((H, 2, 2, TF, W), F32),
                pltpu.VMEM((H, 2, 2, TF, W), F32),
                dma((2, 2, NZ)), dma((2, 2, NZ)),
                dma((H, NZ)), dma((H, NZ)),
                dma((H, NZ)), dma((H, NZ)),
                dma((H,)), dma((H,)),
                dma((H, 2)), dma((H, 2)),
            ],
            compiler_params=pltpu.CompilerParams(
                collective_id=0, has_side_effects=True, vmem_limit_bytes=48 << 20
            ),
        )
        result = call(
            order, counts, neighbours, face_ids,
            rhs[0, 0], inv_blocks[0, 0], coupling, trace_ops, lift_ops,
        )
        return result[None, None]

    placed = (
        P("stream", "span", None, None, None),
        P("stream", "span", None, None, None),
        P(),
        P(),
        P(),
        P("stream", "span", None),
        P("stream", "span"),
        P("stream", "span", None, None),
        P("stream", "span", None, None),
    )
    return jax.shard_map(
        local,
        mesh=mesh,
        in_specs=placed,
        out_specs=P("stream", "span", None, None, None),
        check_vma=False,
    )
```

```python
import functools

import jax
import jax.numpy as jnp
from jax import lax
from jax.experimental import pallas as pl
from jax.experimental.pallas import tpu as pltpu
from jax.sharding import PartitionSpec as P

MESH = pl.DeviceIdType.MESH
F32 = jnp.float32
BF16 = jnp.bfloat16
SWEEPS = 2
B = 320
TF = 80
W = 128


def split(v):
    high = v.astype(BF16)
    return high, (v - high.astype(F32)).astype(BF16)


def apply(operator, v):
    high, low = split(v)
    both = jnp.dot(operator, jnp.concatenate([high, low], axis=1), preferred_element_type=F32)
    return both[:, :W] + both[:, W:]


def nt(a, b):
    return lax.dot_general(a, b, (((1,), (1,)), ((), ())), preferred_element_type=F32)


def through(v, high_map, low_map):
    high, low = split(v)
    rows = v.shape[0]
    both = nt(jnp.concatenate([high, low], axis=0), high_map)
    return both[:rows] + both[rows:] + nt(high, low_map)


def kernel(
    NX, NZ, NS,
    order_hbm, count_hbm, nbr_hbm, fid_hbm, rhs_hbm, inv_hbm, coup_hbm, trop_hbm, liftt_hbm,
    out_ref,
    order_ref, count_ref, nbr_ref, fid_ref, rhs_ref, inv_ref, coup_ref, trop_ref, liftt_ref,
    invs, coups, lpad, ltpad, tpad, base, resid, field,
    tmsg, tmap, prod, dmap, dmsg, dbuf, sstage, sbuf, ostage, wbuf, gstage, gbuf, icur, pstage, pbuf,
    insem, tsend, trecv, asend, arecv, bsend, brecv, gsend, grecv, dsend, drecv, psend, precv,
):
    CH = W // NZ
    i = lax.axis_index("stream")
    j = lax.axis_index("span")
    z = lax.rem(i, NZ)
    x = lax.div(i, NZ)

    def at_z(offset):
        return lax.rem(z + (offset + NZ), NZ)

    def line_z(zz):
        return (x * NZ + zz, j)

    span_left = (i, lax.rem(j + NS - 1, NS))
    span_right = (i, lax.rem(j + 1, NS))

    barrier = pltpu.get_barrier_semaphore()
    greeted = [line_z(at_z(d)) for d in range(1, NZ)] + [span_left, span_right]
    greeted += [(lax.rem(x + e, NX) * NZ + z, j) for e in range(1, NX)]
    for device in greeted:
        pl.semaphore_signal(barrier, inc=1, device_id=device, device_id_type=MESH)

    pairs = (
        (order_hbm, order_ref), (count_hbm, count_ref), (nbr_hbm, nbr_ref), (fid_hbm, fid_ref),
        (inv_hbm, inv_ref), (coup_hbm, coup_ref), (liftt_hbm, liftt_ref), (trop_hbm, trop_ref),
        (rhs_hbm, rhs_ref),
    )
    loads = [pltpu.make_async_copy(src, dst, insem.at[n]) for n, (src, dst) in enumerate(pairs)]
    for load in loads:
        load.start()

    tmap[:, :, :, TF:W, :] = jnp.zeros((2, NZ, 2, W - TF, 2 * W), BF16)
    tmap[:, :, :, W + TF :, :] = jnp.zeros((2, NZ, 2, W - TF, 2 * W), BF16)
    for ref in (prod, dmap):
        ref[...] = jnp.zeros(ref.shape, BF16)
    ltpad[...] = jnp.zeros(ltpad.shape, BF16)
    tpad[...] = jnp.zeros(tpad.shape, BF16)
    row = lax.broadcasted_iota(jnp.int32, (B, B), 0)
    col = lax.broadcasted_iota(jnp.int32, (B, B), 1)
    identity = jnp.where(row == col, 1.0, 0.0).astype(BF16)
    for load in loads:
        load.wait()

    a = order_ref[0, 0, 0]
    b = order_ref[0, 0, 1]
    a_is_0 = a == 0
    live = count_ref[0, 0] > 1
    zero_block = jnp.zeros((B, B), BF16)
    invs[0] = inv_ref[a]
    invs[1] = jnp.where(live, inv_ref[b], zero_block)
    for q in range(4):
        ltpad[q, 0:TF, :] = liftt_ref[q]
        lpad[q] = nt(identity, ltpad[q]).astype(BF16)
    for d in range(2):
        tpad[d, 0:TF, :] = trop_ref[1 - d]
    for pos, slot in ((0, a), (1, b)):
        for m in range(2):
            present = nbr_ref[0, 0, slot, m] < 2
            coups[pos, m] = jnp.where(present, coup_ref[fid_ref[0, 0, slot, m]], zero_block)
        base[pos] = rhs_ref[slot]

    def coupled(pos, v):
        high, low = split(v)
        v2 = jnp.concatenate([high, low], axis=1)
        both = jnp.dot(coups[pos, 0], v2, preferred_element_type=F32) + jnp.dot(
            coups[pos, 1], v2, preferred_element_type=F32
        )
        return both[:, :W] + both[:, W:]

    lane = lax.broadcasted_iota(jnp.int32, (TF, W), 1)

    def own_map(d):
        first, second = (0, 1) if d == 0 else (1, 0)
        u1 = jnp.dot(invs[first], lpad[d], preferred_element_type=F32)
        u2 = jnp.dot(invs[second], lpad[d], preferred_element_type=F32)
        v = apply(invs[second], coupled(second, u1))
        trace = trop_ref[1 - d]
        t11 = -apply(trace, u1)
        t22 = -apply(trace, u2)
        t21 = apply(trace, v)
        first_is_0 = jnp.where(a_is_0, 1.0 - d, 0.0 + d).astype(F32)
        flag = jnp.zeros((TF, W), F32) + first_is_0
        upper = jnp.where(lane < TF, t11, jnp.where(lane < 112, pltpu.roll(t22, 32, 1), flag))
        lower = jnp.where(lane < TF, t21, pltpu.roll(t22, TF, 1))
        tmsg[d, z, 0:TF, :] = upper
        tmsg[d, z, TF : 2 * TF, :] = lower

    def unpack(d, zz):
        p = zz if d == 0 else NZ - 1 - zz
        upper = tmsg[d, zz, 0:TF, :]
        lower = tmsg[d, zz, TF : 2 * TF, :]
        flag = jnp.sum(jnp.where(lane == 120, upper, 0.0), axis=1, keepdims=True) > 0.5
        zero = jnp.zeros((TF, W), F32)
        t11 = jnp.where(lane < TF, upper, zero)
        t21 = jnp.where(lane < TF, lower, zero)
        t22 = jnp.where(
            lane < 48,
            pltpu.roll(lower, 48, 1),
            jnp.where(lane < TF, pltpu.roll(upper, 96, 1), zero),
        )
        blocks = (
            (0, 0, jnp.where(flag, t11, t22)),
            (0, W, jnp.where(flag, zero, t21)),
            (W, 0, jnp.where(flag, t21, zero)),
            (W, W, jnp.where(flag, t22, t11)),
        )
        for row, col, block in blocks:
            high, low = split(block)
            tmap[d, p, 0, row : row + TF, col : col + W] = high
            tmap[d, p, 1, row : row + TF, col : col + W] = low

    reach = (NZ // 2, NZ - 1 - NZ // 2)

    def t_copy(d, ring, k, zz):
        step = 1 if ring == 0 else -1
        return pltpu.make_async_remote_copy(
            src_ref=tmsg.at[d, zz],
            dst_ref=tmsg.at[d, zz],
            send_sem=tsend.at[d, ring, k],
            recv_sem=trecv.at[d, ring, k],
            device_id=line_z(at_z(step)),
            device_id_type=MESH,
        )

    def t_begin(d):
        for ring in range(2):
            if reach[ring] > 0:
                t_copy(d, ring, 0, z).start()

    def t_step(d, k):
        for ring in range(2):
            if k > reach[ring]:
                continue
            source = at_z(-k if ring == 0 else k)
            t_copy(d, ring, k - 1, source).wait_recv()
            if k < reach[ring]:
                t_copy(d, ring, k, source).start()
        for ring in range(2):
            if k <= reach[ring]:
                unpack(d, at_z(-k if ring == 0 else k))

    def t_end(d):
        for ring in range(2):
            for k in range(reach[ring]):
                t_copy(d, ring, k, at_z(-k if ring == 0 else k)).wait_send()

    def multiply(left, right):
        high = jnp.concatenate([left[0, 0:TF, :], left[0, W : W + TF, :]], axis=0)
        low = jnp.concatenate([left[1, 0:TF, :], left[1, W : W + TF, :]], axis=0)
        return (
            jnp.dot(high, right[0], preferred_element_type=F32)
            + jnp.dot(high, right[1], preferred_element_type=F32)
            + jnp.dot(low, right[0], preferred_element_type=F32)
        )

    def keep(ref, value):
        for part, v in enumerate(split(value)):
            ref[part, 0:TF, :] = v[0:TF]
            ref[part, W : W + TF, :] = v[TF:]

    lane_d = lax.broadcasted_iota(jnp.int32, (2 * TF, W), 1)
    lane_q = lax.broadcasted_iota(jnp.int32, (TF // 2, W), 1)

    def d_copy(d, e, device):
        return pltpu.make_async_remote_copy(
            src_ref=dmsg.at[d],
            dst_ref=dbuf.at[d, e],
            send_sem=dsend.at[d, e],
            recv_sem=drecv.at[d, e],
            device_id=device,
            device_id_type=MESH,
        )

    def group_line(d, e):
        return ((x + e if d == 0 else x - e) * NZ + z, j)

    def group_map(d):
        xp = x if d == 0 else NX - 1 - x
        level = [tmap.at[d, p] for p in range(NZ)]
        slot = 0
        while len(level) > 2:
            joined = []
            for n in range(0, len(level), 2):
                keep(prod.at[slot], multiply(level[n + 1], level[n]))
                joined.append(prod.at[slot])
                slot += 1
            level = joined
        total = multiply(level[1], level[0])
        rolled = pltpu.roll(total[:, W:], TF, 1)
        dmsg[d, 0 : 2 * TF, :] = jnp.where(lane_d < TF, total[:, :W], rolled)
        quarter = TF // 2
        rest = rolled[0:quarter]
        for q in range(1, 4):
            rest = jnp.where(
                lane_q < 32 * q, rest, pltpu.roll(rolled[q * quarter : (q + 1) * quarter], 32 * q, 1)
            )
        dmsg[d, 2 * TF :, :] = rest
        for e in range(1, NX - 1):

            @pl.when(jnp.logical_and(xp >= 1, xp + e <= NX - 1))
            def _():
                d_copy(d, e, group_line(d, e)).start()

    def group_arrive(d):
        xp = x if d == 0 else NX - 1 - x
        for source in range(1, NX - 1):

            @pl.when(xp > source)
            def _():
                e = xp - source
                d_copy(d, e, group_line(d, -e)).wait_recv()
                main = dbuf[d, e, 0 : 2 * TF, :]
                rest = dbuf[d, e, 2 * TF :, :]
                spread = jnp.concatenate(
                    [rest] + [pltpu.roll(rest, W - 32 * q, 1) for q in range(1, 4)], axis=0
                )
                zero = jnp.zeros((2 * TF, W), F32)
                left = jnp.where(lane_d < TF, main, zero)
                rolled = jnp.where(lane_d >= TF, main, jnp.where(lane_d < 32, spread, zero))
                right = pltpu.roll(rolled, 48, 1)
                keep(dmap.at[d, source], jnp.concatenate([left, right], axis=1))

    def group_end(d):
        xp = x if d == 0 else NX - 1 - x
        for e in range(1, NX - 1):

            @pl.when(jnp.logical_and(xp >= 1, xp + e <= NX - 1))
            def _():
                d_copy(d, e, group_line(d, e)).wait_send()

    far_first = sorted(range(1, NZ), key=lambda d: (-min(d, NZ - d), d))

    def a_copy(h, d):
        zz = at_z(d)
        return pltpu.make_async_remote_copy(
            src_ref=sstage.at[h, pl.ds(pl.multiple_of(zz * CH, CH), CH), :],
            dst_ref=sbuf.at[h, z],
            send_sem=asend.at[h, d],
            recv_sem=arecv.at[h, d],
            device_id=line_z(zz),
            device_id_type=MESH,
        )

    def b_copy(h, d, p):
        return pltpu.make_async_remote_copy(
            src_ref=ostage.at[h, p],
            dst_ref=wbuf.at[h, pl.ds(pl.multiple_of(z * CH, CH), CH), :],
            send_sem=bsend.at[h, d],
            recv_sem=brecv.at[h, d],
            device_id=line_z(at_z(d)),
            device_id_type=MESH,
        )

    def g_copy(h, e, device):
        return pltpu.make_async_remote_copy(
            src_ref=gstage.at[h],
            dst_ref=gbuf.at[h, e],
            send_sem=gsend.at[h, e],
            recv_sem=grecv.at[h, e],
            device_id=device,
            device_id_type=MESH,
        )

    def p_copy(h, side, device):
        return pltpu.make_async_remote_copy(
            src_ref=pstage.at[h, side],
            dst_ref=pbuf.at[h, side],
            send_sem=psend.at[h, side],
            recv_sem=precv.at[h, side],
            device_id=device,
            device_id_type=MESH,
        )

    def solve(h, d, initial):
        first, second = (0, 1) if d == 0 else (1, 0)
        if initial:
            r1, r2 = base[first], base[second]
        else:
            r1, r2 = resid[first] - coupled(first, field[second]), resid[second]
        x1 = apply(invs[first], r1)
        x2 = apply(invs[second], r2 - coupled(second, x1))
        field[first] = x1
        field[second] = x2
        s1 = apply(tpad[d], x1)
        s2 = apply(tpad[d], x2)
        sa, sb = (s1, s2) if d == 0 else (s2, s1)
        sstage[h, :, 0:W] = jnp.where(a_is_0, sa, sb).T
        sstage[h, :, W : 2 * W] = jnp.where(a_is_0, sb, sa).T
        for dist in far_first:
            a_copy(h, dist).start()
        sbuf[h, z] = sstage[h, pl.ds(pl.multiple_of(z * CH, CH), CH), :]

    def at_start(k, d, action):
        if d == 0:
            pl.when(k == 0)(action)

    def finish(k, d):
        h = 2 * k + d
        first, second = (0, 1) if d == 0 else (1, 0)
        xp = x if d == 0 else NX - 1 - x
        for dist in far_first:
            a_copy(h, dist).wait_recv()

        def line_sum(p):
            return sbuf[h, p if d == 0 else NZ - 1 - p]

        v = line_sum(0)
        for p in range(1, NZ):
            v = through(v, tmap[d, p, 0], tmap[d, p, 1]) + line_sum(p)
        gstage[h] = v
        for e in range(1, NX):

            @pl.when(xp + e <= NX - 1)
            def _():
                g_copy(h, e, group_line(d, e)).start()

        def forward_group():
            group_map(0)
            t_step(1, 1)

        at_start(k, d, forward_group)
        pl.when(k == 0)(lambda: group_arrive(d))
        icur[...] = jnp.zeros((CH, 2 * W), F32)
        for source in range(NX - 1):

            @pl.when(xp > source)
            def _():
                e = xp - source
                g_copy(h, e, group_line(d, -e)).wait_recv()
                if source == 0:
                    icur[...] = gbuf[h, e]
                else:
                    icur[...] = gbuf[h, e] + through(
                        icur[...], dmap[d, source, 0], dmap[d, source, 1]
                    )

        v = icur[...]
        for p in range(NZ):
            ostage[h, p] = v
            if p < NZ - 1:
                v = through(v, tmap[d, p, 0], tmap[d, p, 1]) + line_sum(p)
        for dist in far_first:
            zz = at_z(dist)
            b_copy(h, dist, zz if d == 0 else NZ - 1 - zz).start()
        own = z if d == 0 else NZ - 1 - z
        wbuf[h, pl.ds(pl.multiple_of(z * CH, CH), CH), :] = ostage[h, own]

        def more_maps():
            for n in range(2, NZ // 2):
                t_step(1, n)

        at_start(k, d, more_maps)
        for dist in far_first:
            b_copy(h, dist, 0).wait_recv()

        w0 = wbuf[h, :, 0:W].T
        w1 = wbuf[h, :, W : 2 * W].T
        wa = jnp.where(a_is_0, w0, w1)
        wb = jnp.where(a_is_0, w1, w0)
        lifted = (apply(lpad[d], wa), apply(lpad[d], wb))
        y1 = apply(invs[first], lifted[first])
        y2 = apply(invs[second], lifted[second] - coupled(second, y1))
        x1 = field[first] - y1
        x2 = field[second] - y2
        field[first] = x1
        field[second] = x2

        def exchange():
            xa, xb = (x1, x2) if d == 0 else (x2, x1)
            for side, trace, device in ((0, 3, span_right), (1, 2, span_left)):
                ta = apply(trop_ref[trace], xa)
                tb = apply(trop_ref[trace], xb)
                pstage[h, side, 0] = jnp.where(a_is_0, ta, tb)
                pstage[h, side, 1] = jnp.where(a_is_0, tb, ta)
                p_copy(h, side, device).start()
            for pos in range(2):
                resid[pos] = base[pos] - lifted[pos]

            def last_maps():
                if NZ // 2 > 1:
                    t_step(1, NZ // 2)
                t_end(1)
                group_end(0)

            at_start(k, d, last_maps)
            p_copy(h, 0, span_right).wait_recv()
            p_copy(h, 1, span_left).wait_recv()
            for pos in range(2):
                total = resid[pos]
                for side in range(2):
                    t0 = pbuf[h, side, 0]
                    t1 = pbuf[h, side, 1]
                    mine, other = (t0, t1) if pos == 0 else (t1, t0)
                    total = total - apply(
                        lpad[2 + side, :, 0:TF], jnp.where(a_is_0, mine, other)
                    )
                resid[pos] = total
            p_copy(h, 0, span_right).wait_send()
            p_copy(h, 1, span_left).wait_send()

        if d == 0:
            exchange()
        else:
            pl.when(k < SWEEPS - 1)(exchange)

        for dist in far_first:
            a_copy(h, dist).wait_send()
            b_copy(h, dist, 0).wait_send()
        for e in range(1, NX):

            @pl.when(xp + e <= NX - 1)
            def _():
                g_copy(h, e, group_line(d, e)).wait_send()

    own_map(0)
    pl.semaphore_wait(barrier, len(greeted))
    t_begin(0)
    solve(0, 0, True)
    own_map(1)
    unpack(0, z)
    unpack(1, z)
    for k in range(1, NZ // 2 + 1):
        t_step(0, k)
    t_begin(1)
    t_end(0)

    def sweep(k, carry):
        finish(k, 0)
        solve(2 * k + 1, 1, False)

        @pl.when(k == 0)
        def _():
            group_map(1)

        finish(k, 1)

        @pl.when(k < SWEEPS - 1)
        def _():
            solve(2 * k + 2, 0, False)

        return carry

    lax.fori_loop(0, SWEEPS, sweep, 0)
    group_end(1)
    out_ref[0] = jnp.where(a_is_0, field[0], field[1])
    out_ref[1] = jnp.where(a_is_0, field[1], field[0])


def solution(mesh):
    lines = mesh.shape["stream"]
    NZ = {32: 8, 8: 4, 4: 2}[lines]
    NX = lines // NZ
    NS = mesh.shape["span"]
    CH = W // NZ
    H = 2 * SWEEPS

    def local(rhs, inv_blocks, coupling, trace_ops, lift_ops, order, counts, neighbours, face_ids):
        dma = pltpu.SemaphoreType.DMA
        call = pl.pallas_call(
            functools.partial(kernel, NX, NZ, NS),
            out_shape=jax.ShapeDtypeStruct((2, B, W), F32),
            in_specs=[pl.BlockSpec(memory_space=pl.ANY)] * 9,
            out_specs=pl.BlockSpec(memory_space=pltpu.VMEM),
            scratch_shapes=[
                pltpu.SMEM((1, 1, 2), jnp.int32),
                pltpu.SMEM((1, 1), jnp.int32),
                pltpu.SMEM((1, 1, 2, 2), jnp.int32),
                pltpu.SMEM((1, 1, 2, 2), jnp.int32),
                pltpu.VMEM((2, B, W), F32),
                pltpu.VMEM((2, B, B), BF16),
                pltpu.VMEM((6, B, B), BF16),
                pltpu.VMEM((4, TF, B), BF16),
                pltpu.VMEM((4, TF, B), BF16),
                pltpu.VMEM((2, B, B), BF16),
                pltpu.VMEM((2, 2, B, B), BF16),
                pltpu.VMEM((4, B, W), BF16),
                pltpu.VMEM((4, W, B), BF16),
                pltpu.VMEM((2, W, B), BF16),
                pltpu.VMEM((2, B, W), F32),
                pltpu.VMEM((2, B, W), F32),
                pltpu.VMEM((2, B, W), F32),
                pltpu.VMEM((2, NZ, 2 * TF, W), F32),
                pltpu.VMEM((2, NZ, 2, 2 * W, 2 * W), BF16),
                pltpu.VMEM((NZ, 2, 2 * W, 2 * W), BF16),
                pltpu.VMEM((2, NX, 2, 2 * W, 2 * W), BF16),
                pltpu.VMEM((2, 5 * TF // 2, W), F32),
                pltpu.VMEM((2, NX, 5 * TF // 2, W), F32),
                pltpu.VMEM((H, W, 2 * W), F32),
                pltpu.VMEM((H, NZ, CH, 2 * W), F32),
                pltpu.VMEM((H, NZ, CH, 2 * W), F32),
                pltpu.VMEM((H, W, 2 * W), F32),
                pltpu.VMEM((H, CH, 2 * W), F32),
                pltpu.VMEM((H, NX, CH, 2 * W), F32),
                pltpu.VMEM((CH, 2 * W), F32),
                pltpu.VMEM((H, 2, 2, TF, W), F32),
                pltpu.VMEM((H, 2, 2, TF, W), F32),
                dma((9,)),
                dma((2, 2, NZ)), dma((2, 2, NZ)),
                dma((H, NZ)), dma((H, NZ)),
                dma((H, NZ)), dma((H, NZ)),
                dma((H, NX)), dma((H, NX)),
                dma((2, NX)), dma((2, NX)),
                dma((H, 2)), dma((H, 2)),
            ],
            compiler_params=pltpu.CompilerParams(
                collective_id=0, has_side_effects=True, vmem_limit_bytes=60 << 20
            ),
        )
        result = call(
            order, counts, neighbours, face_ids,
            rhs[0, 0], inv_blocks[0, 0], coupling, trace_ops, lift_ops.transpose(0, 2, 1),
        )
        return result[None, None]

    placed = (
        P("stream", "span", None, None, None),
        P("stream", "span", None, None, None),
        P(),
        P(),
        P(),
        P("stream", "span", None),
        P("stream", "span"),
        P("stream", "span", None, None),
        P("stream", "span", None, None),
    )
    return jax.shard_map(
        local,
        mesh=mesh,
        in_specs=placed,
        out_specs=P("stream", "span", None, None, None),
        check_vma=False,
    )
```

```python
import functools

import jax
import jax.numpy as jnp
from jax import lax
from jax.experimental import pallas as pl
from jax.experimental.pallas import tpu as pltpu
from jax.sharding import PartitionSpec as P

MESH = pl.DeviceIdType.MESH
F32 = jnp.float32
BF16 = jnp.bfloat16
SWEEPS = 2
B = 320
TF = 80
W = 128


def split(v):
    high = v.astype(BF16)
    return high, (v - high.astype(F32)).astype(BF16)


def apply(operator, v):
    high, low = split(v)
    both = jnp.dot(operator, jnp.concatenate([high, low], axis=1), preferred_element_type=F32)
    return both[:, :W] + both[:, W:]


def nt(a, b):
    return lax.dot_general(a, b, (((1,), (1,)), ((), ())), preferred_element_type=F32)


def through(v, high_map, low_map):
    high, low = split(v)
    rows = v.shape[0]
    both = nt(jnp.concatenate([high, low], axis=0), high_map)
    return both[:rows] + both[rows:] + nt(high, low_map)


def kernel(
    NX, NZ, NS,
    order_hbm, count_hbm, nbr_hbm, fid_hbm, rhs_hbm, inv_hbm, coup_hbm, trop_hbm, liftt_hbm,
    out_ref,
    order_ref, count_ref, nbr_ref, fid_ref, rhs_ref, inv_ref, coup_ref, trop_ref, liftt_ref,
    invs, coups, lpad, ltpad, tpad, base, resid, field,
    kept, wmap, nmap, tloc, tfull, spar,
    tmsg, tmap, prod, dmap, dmsg, dbuf, sstage, sbuf, ostage, wbuf, gstage, gbuf, icur, pstage, pbuf,
    insem, tsend, trecv, asend, arecv, bsend, brecv, gsend, grecv, dsend, drecv, psend, precv,
):
    CH = W // NZ
    i = lax.axis_index("stream")
    j = lax.axis_index("span")
    z = lax.rem(i, NZ)
    x = lax.div(i, NZ)

    def at_z(offset):
        return lax.rem(z + (offset + NZ), NZ)

    def line_z(zz):
        return (x * NZ + zz, j)

    span_left = (i, lax.rem(j + NS - 1, NS))
    span_right = (i, lax.rem(j + 1, NS))

    barrier = pltpu.get_barrier_semaphore()
    greeted = [line_z(at_z(d)) for d in range(1, NZ)] + [span_left, span_right]
    greeted += [(lax.rem(x + e, NX) * NZ + z, j) for e in range(1, NX)]
    for device in greeted:
        pl.semaphore_signal(barrier, inc=1, device_id=device, device_id_type=MESH)

    pairs = (
        (order_hbm, order_ref), (count_hbm, count_ref), (nbr_hbm, nbr_ref), (fid_hbm, fid_ref),
        (inv_hbm, inv_ref), (coup_hbm, coup_ref), (liftt_hbm, liftt_ref), (trop_hbm, trop_ref),
        (rhs_hbm, rhs_ref),
    )
    loads = [pltpu.make_async_copy(src, dst, insem.at[n]) for n, (src, dst) in enumerate(pairs)]
    for load in loads:
        load.start()

    tmap[:, :, :, TF:W, :] = jnp.zeros((2, NZ, 2, W - TF, 2 * W), BF16)
    tmap[:, :, :, W + TF :, :] = jnp.zeros((2, NZ, 2, W - TF, 2 * W), BF16)
    tfull[...] = jnp.zeros(tfull.shape, F32)
    for ref in (prod, dmap, wmap, nmap):
        ref[...] = jnp.zeros(ref.shape, BF16)
    ltpad[...] = jnp.zeros(ltpad.shape, BF16)
    tpad[...] = jnp.zeros(tpad.shape, BF16)
    row = lax.broadcasted_iota(jnp.int32, (B, B), 0)
    col = lax.broadcasted_iota(jnp.int32, (B, B), 1)
    identity = jnp.where(row == col, 1.0, 0.0).astype(BF16)
    for load in loads:
        load.wait()

    a = order_ref[0, 0, 0]
    b = order_ref[0, 0, 1]
    a_is_0 = a == 0
    live = count_ref[0, 0] > 1
    zero_block = jnp.zeros((B, B), BF16)
    invs[0] = inv_ref[a]
    invs[1] = jnp.where(live, inv_ref[b], zero_block)
    for q in range(4):
        ltpad[q, 0:TF, :] = liftt_ref[q]
        lpad[q] = nt(identity, ltpad[q]).astype(BF16)
    for d in range(2):
        tpad[d, 0:TF, :] = trop_ref[1 - d]
    for pos, slot in ((0, a), (1, b)):
        for m in range(2):
            present = nbr_ref[0, 0, slot, m] < 2
            coups[pos, m] = jnp.where(present, coup_ref[fid_ref[0, 0, slot, m]], zero_block)
        base[pos] = rhs_ref[slot]

    def coupled(pos, v):
        high, low = split(v)
        v2 = jnp.concatenate([high, low], axis=1)
        both = jnp.dot(coups[pos, 0], v2, preferred_element_type=F32) + jnp.dot(
            coups[pos, 1], v2, preferred_element_type=F32
        )
        return both[:, :W] + both[:, W:]

    lane = lax.broadcasted_iota(jnp.int32, (TF, W), 1)

    def response(d, q):
        first, second = (0, 1) if d == 0 else (1, 0)
        u1 = jnp.dot(invs[first], lpad[q], preferred_element_type=F32)
        u2 = jnp.dot(invs[second], lpad[q], preferred_element_type=F32)
        v = apply(invs[second], coupled(second, u1))
        return u1, u2, v

    def own_map(d):
        u1, u2, v = response(d, d)
        for n, part in enumerate((u1, u2, v)):
            kept[d, n] = part
        trace = trop_ref[1 - d]
        t11 = -apply(trace, u1)
        t22 = -apply(trace, u2)
        t21 = apply(trace, v)
        first_is_0 = jnp.where(a_is_0, 1.0 - d, 0.0 + d).astype(F32)
        flag = jnp.zeros((TF, W), F32) + first_is_0
        upper = jnp.where(lane < TF, t11, jnp.where(lane < 112, pltpu.roll(t22, 32, 1), flag))
        lower = jnp.where(lane < TF, t21, pltpu.roll(t22, TF, 1))
        tmsg[d, z, 0:TF, :] = upper
        tmsg[d, z, TF : 2 * TF, :] = lower

    def put(ref, row, col, value):
        for part, v in enumerate(split(value)):
            ref[part, row : row + value.shape[0], col : col + W] = v

    def mapped(ref, v):
        high, low = split(v)
        both = jnp.concatenate([high, low], axis=1)
        y = jnp.dot(ref[0], both, preferred_element_type=F32)
        y = y[:, :W] + y[:, W:]
        return y + jnp.dot(ref[1], high, preferred_element_type=F32)

    def span_map(d):
        first, second = (0, 1) if d == 0 else (1, 0)
        for side, face in ((0, 3), (1, 2)):
            trace = trop_ref[face]
            rows = (2 * side + first) * TF, (2 * side + second) * TF
            put(wmap.at[d], rows[0], first * W, apply(trace, kept[d, 0]))
            put(wmap.at[d], rows[1], second * W, apply(trace, kept[d, 1]))
            put(wmap.at[d], rows[1], first * W, -apply(trace, kept[d, 2]))

    def entry_map(d):
        first, second = (0, 1) if d == 0 else (1, 0)
        for side in range(2):
            u1, u2, v = response(d, 2 + side)
            col = 2 * side * W
            put(nmap.at[d], first * W, col + first * W, -apply(tpad[d], u1))
            put(nmap.at[d], second * W, col + second * W, -apply(tpad[d], u2))
            put(nmap.at[d], second * W, col + first * W, apply(tpad[d], v))

    def unpack(d, zz):
        p = zz if d == 0 else NZ - 1 - zz
        upper = tmsg[d, zz, 0:TF, :]
        lower = tmsg[d, zz, TF : 2 * TF, :]
        flag = jnp.sum(jnp.where(lane == 120, upper, 0.0), axis=1, keepdims=True) > 0.5
        zero = jnp.zeros((TF, W), F32)
        t11 = jnp.where(lane < TF, upper, zero)
        t21 = jnp.where(lane < TF, lower, zero)
        t22 = jnp.where(
            lane < 48,
            pltpu.roll(lower, 48, 1),
            jnp.where(lane < TF, pltpu.roll(upper, 96, 1), zero),
        )
        blocks = (
            (0, 0, jnp.where(flag, t11, t22)),
            (0, W, jnp.where(flag, zero, t21)),
            (W, 0, jnp.where(flag, t21, zero)),
            (W, W, jnp.where(flag, t22, t11)),
        )
        for row, col, block in blocks:
            high, low = split(block)
            tmap[d, p, 0, row : row + TF, col : col + W] = high
            tmap[d, p, 1, row : row + TF, col : col + W] = low

    reach = (NZ // 2, NZ - 1 - NZ // 2)

    def t_copy(d, ring, k, zz, half):
        step = 1 if ring == 0 else -1
        rows = pl.ds(half * TF, TF)
        return pltpu.make_async_remote_copy(
            src_ref=tmsg.at[d, zz, rows, :],
            dst_ref=tmsg.at[d, zz, rows, :],
            send_sem=tsend.at[d, ring, k, half],
            recv_sem=trecv.at[d, ring, k, half],
            device_id=line_z(at_z(step)),
            device_id_type=MESH,
        )

    def t_begin(d):
        for half in range(2):
            for ring in range(2):
                if reach[ring] > 0:
                    t_copy(d, ring, 0, z, half).start()

    def t_step(d, k):
        for half in range(2):
            for ring in range(2):
                if k > reach[ring]:
                    continue
                source = at_z(-k if ring == 0 else k)
                t_copy(d, ring, k - 1, source, half).wait_recv()
                if k < reach[ring]:
                    t_copy(d, ring, k, source, half).start()
        for ring in range(2):
            if k <= reach[ring]:
                unpack(d, at_z(-k if ring == 0 else k))

    def t_end(d):
        for ring in range(2):
            for k in range(reach[ring]):
                for half in range(2):
                    t_copy(d, ring, k, at_z(-k if ring == 0 else k), half).wait_send()

    def multiply(left, right):
        high = jnp.concatenate([left[0, 0:TF, :], left[0, W : W + TF, :]], axis=0)
        low = jnp.concatenate([left[1, 0:TF, :], left[1, W : W + TF, :]], axis=0)
        return (
            jnp.dot(high, right[0], preferred_element_type=F32)
            + jnp.dot(high, right[1], preferred_element_type=F32)
            + jnp.dot(low, right[0], preferred_element_type=F32)
        )

    def keep(ref, value):
        for part, v in enumerate(split(value)):
            ref[part, 0:TF, :] = v[0:TF]
            ref[part, W : W + TF, :] = v[TF:]

    lane_d = lax.broadcasted_iota(jnp.int32, (2 * TF, W), 1)
    lane_q = lax.broadcasted_iota(jnp.int32, (TF // 2, W), 1)

    def d_copy(d, e, device):
        return pltpu.make_async_remote_copy(
            src_ref=dmsg.at[d],
            dst_ref=dbuf.at[d, e],
            send_sem=dsend.at[d, e],
            recv_sem=drecv.at[d, e],
            device_id=device,
            device_id_type=MESH,
        )

    def group_line(d, e):
        return ((x + e if d == 0 else x - e) * NZ + z, j)

    def group_map(d):
        xp = x if d == 0 else NX - 1 - x
        level = [tmap.at[d, p] for p in range(NZ)]
        slot = 0
        while len(level) > 2:
            joined = []
            for n in range(0, len(level), 2):
                keep(prod.at[slot], multiply(level[n + 1], level[n]))
                joined.append(prod.at[slot])
                slot += 1
            level = joined
        total = multiply(level[1], level[0])
        rolled = pltpu.roll(total[:, W:], TF, 1)
        dmsg[d, 0 : 2 * TF, :] = jnp.where(lane_d < TF, total[:, :W], rolled)
        quarter = TF // 2
        rest = rolled[0:quarter]
        for q in range(1, 4):
            rest = jnp.where(
                lane_q < 32 * q, rest, pltpu.roll(rolled[q * quarter : (q + 1) * quarter], 32 * q, 1)
            )
        dmsg[d, 2 * TF :, :] = rest
        for e in range(1, NX - 1):

            @pl.when(jnp.logical_and(xp >= 1, xp + e <= NX - 1))
            def _():
                d_copy(d, e, group_line(d, e)).start()

    def group_arrive(d):
        xp = x if d == 0 else NX - 1 - x
        for source in range(1, NX - 1):

            @pl.when(xp > source)
            def _():
                e = xp - source
                d_copy(d, e, group_line(d, -e)).wait_recv()
                main = dbuf[d, e, 0 : 2 * TF, :]
                rest = dbuf[d, e, 2 * TF :, :]
                spread = jnp.concatenate(
                    [rest] + [pltpu.roll(rest, W - 32 * q, 1) for q in range(1, 4)], axis=0
                )
                zero = jnp.zeros((2 * TF, W), F32)
                left = jnp.where(lane_d < TF, main, zero)
                rolled = jnp.where(lane_d >= TF, main, jnp.where(lane_d < 32, spread, zero))
                right = pltpu.roll(rolled, 48, 1)
                keep(dmap.at[d, source], jnp.concatenate([left, right], axis=1))

    def group_end(d):
        xp = x if d == 0 else NX - 1 - x
        for e in range(1, NX - 1):

            @pl.when(jnp.logical_and(xp >= 1, xp + e <= NX - 1))
            def _():
                d_copy(d, e, group_line(d, e)).wait_send()

    far_first = sorted(range(1, NZ), key=lambda d: (-min(d, NZ - d), d))

    def a_copy(h, d):
        zz = at_z(d)
        return pltpu.make_async_remote_copy(
            src_ref=sstage.at[h, pl.ds(pl.multiple_of(zz * CH, CH), CH), :],
            dst_ref=sbuf.at[h, z],
            send_sem=asend.at[h, d],
            recv_sem=arecv.at[h, d],
            device_id=line_z(zz),
            device_id_type=MESH,
        )

    def b_copy(h, d, p):
        return pltpu.make_async_remote_copy(
            src_ref=ostage.at[h, p],
            dst_ref=wbuf.at[h, pl.ds(pl.multiple_of(z * CH, CH), CH), :],
            send_sem=bsend.at[h, d],
            recv_sem=brecv.at[h, d],
            device_id=line_z(at_z(d)),
            device_id_type=MESH,
        )

    def g_copy(h, e, device):
        return pltpu.make_async_remote_copy(
            src_ref=gstage.at[h],
            dst_ref=gbuf.at[h, e],
            send_sem=gsend.at[h, e],
            recv_sem=grecv.at[h, e],
            device_id=device,
            device_id_type=MESH,
        )

    def p_copy(h, side, device):
        return pltpu.make_async_remote_copy(
            src_ref=pstage.at[h, side],
            dst_ref=pbuf.at[h, side],
            send_sem=psend.at[h, side],
            recv_sem=precv.at[h, side],
            device_id=device,
            device_id_type=MESH,
        )

    def solve(d, initial):
        first, second = (0, 1) if d == 0 else (1, 0)
        if initial:
            r1, r2 = base[first], base[second]
        else:
            r1, r2 = resid[first] - coupled(first, field[second]), resid[second]
        x1 = apply(invs[first], r1)
        x2 = apply(invs[second], r2 - coupled(second, x1))
        field[first] = x1
        field[second] = x2
        spar[first * W : first * W + W, :] = apply(tpad[d], x1)
        spar[second * W : second * W + W, :] = apply(tpad[d], x2)

    def send_line_traces(h, s):
        sa, sb = s[0:W], s[W:]
        sstage[h, :, 0:W] = jnp.where(a_is_0, sa, sb).T
        sstage[h, :, W : 2 * W] = jnp.where(a_is_0, sb, sa).T
        for dist in far_first:
            a_copy(h, dist).start()
        sbuf[h, z] = sstage[h, pl.ds(pl.multiple_of(z * CH, CH), CH), :]

    def local_span_traces():
        for side, face in ((0, 3), (1, 2)):
            for pos in range(2):
                row = (2 * side + pos) * TF
                tloc[row : row + TF, :] = apply(trop_ref[face], field[pos])

    def at_start(k, d, action):
        if d == 0:
            pl.when(k == 0)(action)

    def finish(k, d):
        h = 2 * k + d
        first, second = (0, 1) if d == 0 else (1, 0)
        xp = x if d == 0 else NX - 1 - x
        for dist in far_first:
            a_copy(h, dist).wait_recv()

        def line_sum(p):
            return sbuf[h, p if d == 0 else NZ - 1 - p]

        v = line_sum(0)
        for p in range(1, NZ):
            v = through(v, tmap[d, p, 0], tmap[d, p, 1]) + line_sum(p)
        gstage[h] = v
        for e in range(1, NX):

            @pl.when(xp + e <= NX - 1)
            def _():
                g_copy(h, e, group_line(d, e)).start()

        def forward_group():
            group_map(0)
            t_step(1, 1)

        at_start(k, d, forward_group)
        pl.when(k == 0)(lambda: group_arrive(d))
        icur[...] = jnp.zeros((CH, 2 * W), F32)
        for source in range(NX - 1):

            @pl.when(xp > source)
            def _():
                e = xp - source
                g_copy(h, e, group_line(d, -e)).wait_recv()
                if source == 0:
                    icur[...] = gbuf[h, e]
                else:
                    icur[...] = gbuf[h, e] + through(
                        icur[...], dmap[d, source, 0], dmap[d, source, 1]
                    )

        v = icur[...]
        for p in range(NZ):
            ostage[h, p] = v
            if p < NZ - 1:
                v = through(v, tmap[d, p, 0], tmap[d, p, 1]) + line_sum(p)
        for dist in far_first:
            zz = at_z(dist)
            b_copy(h, dist, zz if d == 0 else NZ - 1 - zz).start()
        own = z if d == 0 else NZ - 1 - z
        wbuf[h, pl.ds(pl.multiple_of(z * CH, CH), CH), :] = ostage[h, own]

        def more_maps():
            for n in range(2, NZ // 2):
                t_step(1, n)
            entry_map(0)

        at_start(k, d, more_maps)
        for dist in far_first:
            b_copy(h, dist, 0).wait_recv()

        w0 = wbuf[h, :, 0:W].T
        w1 = wbuf[h, :, W : 2 * W].T
        wa = jnp.where(a_is_0, w0, w1)
        wb = jnp.where(a_is_0, w1, w0)
        sides = ((0, span_right), (1, span_left))

        def send_span_traces():
            t = tloc[...] - mapped(wmap.at[d], jnp.concatenate([wa, wb], axis=0))
            for side, device in sides:
                ta = t[2 * side * TF : (2 * side + 1) * TF]
                tb = t[(2 * side + 1) * TF : (2 * side + 2) * TF]
                pstage[h, side, 0] = jnp.where(a_is_0, ta, tb)
                pstage[h, side, 1] = jnp.where(a_is_0, tb, ta)
                p_copy(h, side, device).start()

        def prepare_next():
            for pos in range(2):
                resid[pos] = base[pos] - lifted[pos]
            solve(1 - d, False)

            def last_maps():
                if NZ // 2 > 1:
                    t_step(1, NZ // 2)
                t_end(1)
                group_end(0)

            at_start(k, d, last_maps)
            for side, device in sides:
                p_copy(h, side, device).wait_recv()
                t0 = pbuf[h, side, 0]
                t1 = pbuf[h, side, 1]
                row = 2 * side * W
                tfull[row : row + TF, :] = jnp.where(a_is_0, t0, t1)
                tfull[row + W : row + W + TF, :] = jnp.where(a_is_0, t1, t0)
            send_line_traces(h + 1, spar[...] + mapped(nmap.at[1 - d], tfull[...]))
            taken = [
                apply(lpad[2], tfull[pos * W : pos * W + W, :])
                + apply(lpad[3], tfull[(2 + pos) * W : (2 + pos) * W + W, :])
                for pos in range(2)
            ]
            z1 = apply(invs[second], taken[second])
            z2 = apply(invs[first], taken[first] - coupled(first, z1))
            field[second] = field[second] - z1
            field[first] = field[first] - z2
            local_span_traces()
            for side, device in sides:
                p_copy(h, side, device).wait_send()

        more = d == 0
        if more:
            send_span_traces()
        else:
            pl.when(k < SWEEPS - 1)(send_span_traces)
        lifted = (apply(lpad[d], wa), apply(lpad[d], wb))
        y1 = apply(invs[first], lifted[first])
        y2 = apply(invs[second], lifted[second] - coupled(second, y1))
        field[first] = field[first] - y1
        field[second] = field[second] - y2
        if more:
            prepare_next()
        else:
            pl.when(k < SWEEPS - 1)(prepare_next)

        for dist in far_first:
            a_copy(h, dist).wait_send()
            b_copy(h, dist, 0).wait_send()
        for e in range(1, NX):

            @pl.when(xp + e <= NX - 1)
            def _():
                g_copy(h, e, group_line(d, e)).wait_send()

    own_map(0)
    pl.semaphore_wait(barrier, len(greeted))
    t_begin(0)
    solve(0, True)
    send_line_traces(0, spar[...])
    own_map(1)
    unpack(0, z)
    chunks = [
        lambda: (span_map(0), unpack(1, z), local_span_traces()),
        lambda: entry_map(1),
        lambda: span_map(1),
    ]
    for k in range(1, NZ // 2 + 1):
        t_step(0, k)
        for chunk in chunks[:1] if k < NZ // 2 else chunks:
            chunk()
        chunks = chunks[1:]
    t_begin(1)
    t_end(0)

    def sweep(k, carry):
        finish(k, 0)

        @pl.when(k == 0)
        def _():
            group_map(1)

        finish(k, 1)
        return carry

    lax.fori_loop(0, SWEEPS, sweep, 0)
    group_end(1)
    out_ref[0] = jnp.where(a_is_0, field[0], field[1])
    out_ref[1] = jnp.where(a_is_0, field[1], field[0])


def solution(mesh):
    lines = mesh.shape["stream"]
    NZ = {32: 8, 8: 4, 4: 2}[lines]
    NX = lines // NZ
    NS = mesh.shape["span"]
    CH = W // NZ
    H = 2 * SWEEPS

    def local(rhs, inv_blocks, coupling, trace_ops, lift_ops, order, counts, neighbours, face_ids):
        dma = pltpu.SemaphoreType.DMA
        call = pl.pallas_call(
            functools.partial(kernel, NX, NZ, NS),
            out_shape=jax.ShapeDtypeStruct((2, B, W), F32),
            in_specs=[pl.BlockSpec(memory_space=pl.ANY)] * 9,
            out_specs=pl.BlockSpec(memory_space=pltpu.VMEM),
            scratch_shapes=[
                pltpu.SMEM((1, 1, 2), jnp.int32),
                pltpu.SMEM((1, 1), jnp.int32),
                pltpu.SMEM((1, 1, 2, 2), jnp.int32),
                pltpu.SMEM((1, 1, 2, 2), jnp.int32),
                pltpu.VMEM((2, B, W), F32),
                pltpu.VMEM((2, B, B), BF16),
                pltpu.VMEM((6, B, B), BF16),
                pltpu.VMEM((4, TF, B), BF16),
                pltpu.VMEM((4, TF, B), BF16),
                pltpu.VMEM((2, B, B), BF16),
                pltpu.VMEM((2, 2, B, B), BF16),
                pltpu.VMEM((4, B, W), BF16),
                pltpu.VMEM((4, W, B), BF16),
                pltpu.VMEM((2, W, B), BF16),
                pltpu.VMEM((2, B, W), F32),
                pltpu.VMEM((2, B, W), F32),
                pltpu.VMEM((2, B, W), F32),
                pltpu.VMEM((2, 3, B, W), F32),
                pltpu.VMEM((2, 2, 4 * TF, 2 * W), BF16),
                pltpu.VMEM((2, 2, 2 * W, 4 * W), BF16),
                pltpu.VMEM((4 * TF, W), F32),
                pltpu.VMEM((4 * W, W), F32),
                pltpu.VMEM((2 * W, W), F32),
                pltpu.VMEM((2, NZ, 2 * TF, W), F32),
                pltpu.VMEM((2, NZ, 2, 2 * W, 2 * W), BF16),
                pltpu.VMEM((NZ, 2, 2 * W, 2 * W), BF16),
                pltpu.VMEM((2, NX, 2, 2 * W, 2 * W), BF16),
                pltpu.VMEM((2, 5 * TF // 2, W), F32),
                pltpu.VMEM((2, NX, 5 * TF // 2, W), F32),
                pltpu.VMEM((H, W, 2 * W), F32),
                pltpu.VMEM((H, NZ, CH, 2 * W), F32),
                pltpu.VMEM((H, NZ, CH, 2 * W), F32),
                pltpu.VMEM((H, W, 2 * W), F32),
                pltpu.VMEM((H, CH, 2 * W), F32),
                pltpu.VMEM((H, NX, CH, 2 * W), F32),
                pltpu.VMEM((CH, 2 * W), F32),
                pltpu.VMEM((H, 2, 2, TF, W), F32),
                pltpu.VMEM((H, 2, 2, TF, W), F32),
                dma((9,)),
                dma((2, 2, NZ, 2)), dma((2, 2, NZ, 2)),
                dma((H, NZ)), dma((H, NZ)),
                dma((H, NZ)), dma((H, NZ)),
                dma((H, NX)), dma((H, NX)),
                dma((2, NX)), dma((2, NX)),
                dma((H, 2)), dma((H, 2)),
            ],
            compiler_params=pltpu.CompilerParams(
                collective_id=0, has_side_effects=True, vmem_limit_bytes=60 << 20
            ),
        )
        result = call(
            order, counts, neighbours, face_ids,
            rhs[0, 0], inv_blocks[0, 0], coupling, trace_ops, lift_ops.transpose(0, 2, 1),
        )
        return result[None, None]

    placed = (
        P("stream", "span", None, None, None),
        P("stream", "span", None, None, None),
        P(),
        P(),
        P(),
        P("stream", "span", None),
        P("stream", "span"),
        P("stream", "span", None, None),
        P("stream", "span", None, None),
    )
    return jax.shard_map(
        local,
        mesh=mesh,
        in_specs=placed,
        out_specs=P("stream", "span", None, None, None),
        check_vma=False,
    )
```

```python
import functools

import jax
import jax.numpy as jnp
from jax import lax
from jax.experimental import pallas as pl
from jax.experimental.pallas import tpu as pltpu
from jax.sharding import PartitionSpec as P

MESH = pl.DeviceIdType.MESH
F32 = jnp.float32
BF16 = jnp.bfloat16
SWEEPS = 2
B = 320
TF = 80
W = 128


def split(v):
    high = v.astype(BF16)
    return high, (v - high.astype(F32)).astype(BF16)


def apply(operator, v):
    high, low = split(v)
    both = jnp.dot(operator, jnp.concatenate([high, low], axis=1), preferred_element_type=F32)
    return both[:, :W] + both[:, W:]


def nt(a, b):
    return lax.dot_general(a, b, (((1,), (1,)), ((), ())), preferred_element_type=F32)


def through(v, high_map, low_map):
    high, low = split(v)
    rows = v.shape[0]
    both = nt(jnp.concatenate([high, low], axis=0), high_map)
    return both[:rows] + both[rows:] + nt(high, low_map)


def kernel(
    NX, NZ, NS,
    order_hbm, count_hbm, nbr_hbm, fid_hbm, rhs_hbm, inv_hbm, coup_hbm, trop_hbm, liftt_hbm,
    out_ref,
    order_ref, count_ref, nbr_ref, fid_ref, rhs_ref, inv_ref, coup_ref, trop_ref, liftt_ref,
    invs, coups, lpad, ltpad, tpad, base, resid, field,
    kept, wmap, nmap, tloc, tfull, spar,
    tmsg, tmap, prod, dmap, dmsg, dbuf, sstage, sbuf, lsum, ostage, wbuf, gstage, gbuf, icur, pstage, pbuf,
    insem, tsend, trecv, asend, arecv, bsend, brecv, gsend, grecv, dsend, drecv, psend, precv,
):
    CH = W // NZ
    i = lax.axis_index("stream")
    j = lax.axis_index("span")
    z = lax.rem(i, NZ)
    x = lax.div(i, NZ)

    def at_z(offset):
        return lax.rem(z + (offset + NZ), NZ)

    def line_z(zz):
        return (x * NZ + zz, j)

    span_left = (i, lax.rem(j + NS - 1, NS))
    span_right = (i, lax.rem(j + 1, NS))

    barrier = pltpu.get_barrier_semaphore()
    greeted = [line_z(at_z(d)) for d in range(1, NZ)] + [span_left, span_right]
    greeted += [(lax.rem(x + e, NX) * NZ + z, j) for e in range(1, NX)]
    for device in greeted:
        pl.semaphore_signal(barrier, inc=1, device_id=device, device_id_type=MESH)

    pairs = (
        (order_hbm, order_ref), (count_hbm, count_ref), (nbr_hbm, nbr_ref), (fid_hbm, fid_ref),
        (inv_hbm, inv_ref), (coup_hbm, coup_ref), (liftt_hbm, liftt_ref), (trop_hbm, trop_ref),
        (rhs_hbm, rhs_ref),
    )
    loads = [pltpu.make_async_copy(src, dst, insem.at[n]) for n, (src, dst) in enumerate(pairs)]
    for load in loads:
        load.start()

    tmap[:, :, :, TF:W, :] = jnp.zeros((2, NZ, 2, W - TF, 2 * W), BF16)
    tmap[:, :, :, W + TF :, :] = jnp.zeros((2, NZ, 2, W - TF, 2 * W), BF16)
    tfull[...] = jnp.zeros(tfull.shape, F32)
    for ref in (wmap, nmap):
        ref[...] = jnp.zeros(ref.shape, BF16)
    gap = W - TF
    for d in range(2):
        for rows in (pl.ds(TF, gap), pl.ds(W + TF, gap)):
            prod[d, :, :, rows, :] = jnp.zeros((prod.shape[1], 2, gap, 2 * W), BF16)
            dmap[d, :, :, rows, :] = jnp.zeros((dmap.shape[1], 2, gap, 2 * W), BF16)
    ltpad[...] = jnp.zeros(ltpad.shape, BF16)
    tpad[...] = jnp.zeros(tpad.shape, BF16)
    row = lax.broadcasted_iota(jnp.int32, (B, B), 0)
    col = lax.broadcasted_iota(jnp.int32, (B, B), 1)
    identity = jnp.where(row == col, 1.0, 0.0).astype(BF16)
    for load in loads[:-1]:
        load.wait()

    a = order_ref[0, 0, 0]
    b = order_ref[0, 0, 1]
    a_is_0 = a == 0
    live = count_ref[0, 0] > 1
    zero_block = jnp.zeros((B, B), BF16)
    invs[0] = inv_ref[a]
    invs[1] = jnp.where(live, inv_ref[b], zero_block)

    def take_lift(q):
        ltpad[q, 0:TF, :] = liftt_ref[q]
        lpad[q] = nt(identity, ltpad[q]).astype(BF16)

    def take_coupling(pos, slot):
        for m in range(2):
            present = nbr_ref[0, 0, slot, m] < 2
            coups[pos, m] = jnp.where(present, coup_ref[fid_ref[0, 0, slot, m]], zero_block)

    def coupled(pos, v):
        high, low = split(v)
        v2 = jnp.concatenate([high, low], axis=1)
        both = jnp.dot(coups[pos, 0], v2, preferred_element_type=F32) + jnp.dot(
            coups[pos, 1], v2, preferred_element_type=F32
        )
        return both[:, :W] + both[:, W:]

    lane = lax.broadcasted_iota(jnp.int32, (TF, W), 1)

    def response(d, q):
        first, second = (0, 1) if d == 0 else (1, 0)
        u1 = jnp.dot(invs[first], lpad[q], preferred_element_type=F32)
        u2 = jnp.dot(invs[second], lpad[q], preferred_element_type=F32)
        v = apply(invs[second], coupled(second, u1))
        return u1, u2, v

    def own_map(d):
        u1, u2, v = response(d, d)
        for n, part in enumerate((u1, u2, v)):
            kept[d, n] = part
        trace = trop_ref[1 - d]
        t11 = -apply(trace, u1)
        t22 = -apply(trace, u2)
        t21 = apply(trace, v)
        first_is_0 = jnp.where(a_is_0, 1.0 - d, 0.0 + d).astype(F32)
        flag = jnp.zeros((TF, W), F32) + first_is_0
        upper = jnp.where(lane < TF, t11, jnp.where(lane < 112, pltpu.roll(t22, 32, 1), flag))
        lower = jnp.where(lane < TF, t21, pltpu.roll(t22, TF, 1))
        tmsg[d, z, 0:TF, :] = upper
        tmsg[d, z, TF : 2 * TF, :] = lower

    def put(ref, row, col, value):
        for part, v in enumerate(split(value)):
            ref[part, row : row + value.shape[0], col : col + W] = v

    def mapped(ref, v):
        high, low = split(v)
        both = jnp.concatenate([high, low], axis=1)
        y = jnp.dot(ref[0], both, preferred_element_type=F32)
        y = y[:, :W] + y[:, W:]
        return y + jnp.dot(ref[1], high, preferred_element_type=F32)

    def span_map(d):
        first, second = (0, 1) if d == 0 else (1, 0)
        for side, face in ((0, 3), (1, 2)):
            trace = trop_ref[face]
            rows = (2 * side + first) * TF, (2 * side + second) * TF
            put(wmap.at[d], rows[0], first * W, apply(trace, kept[d, 0]))
            put(wmap.at[d], rows[1], second * W, apply(trace, kept[d, 1]))
            put(wmap.at[d], rows[1], first * W, -apply(trace, kept[d, 2]))

    def entry_map(d):
        first, second = (0, 1) if d == 0 else (1, 0)
        for side in range(2):
            u1, u2, v = response(d, 2 + side)
            col = 2 * side * W
            put(nmap.at[d], first * W, col + first * W, -apply(tpad[d], u1))
            put(nmap.at[d], second * W, col + second * W, -apply(tpad[d], u2))
            put(nmap.at[d], second * W, col + first * W, apply(tpad[d], v))

    def unpack(d, zz):
        p = zz if d == 0 else NZ - 1 - zz
        upper = tmsg[d, zz, 0:TF, :]
        lower = tmsg[d, zz, TF : 2 * TF, :]
        flag = jnp.sum(jnp.where(lane == 120, upper, 0.0), axis=1, keepdims=True) > 0.5
        zero = jnp.zeros((TF, W), F32)
        t11 = jnp.where(lane < TF, upper, zero)
        t21 = jnp.where(lane < TF, lower, zero)
        t22 = jnp.where(
            lane < 48,
            pltpu.roll(lower, 48, 1),
            jnp.where(lane < TF, pltpu.roll(upper, 96, 1), zero),
        )
        blocks = (
            (0, 0, jnp.where(flag, t11, t22)),
            (0, W, jnp.where(flag, zero, t21)),
            (W, 0, jnp.where(flag, t21, zero)),
            (W, W, jnp.where(flag, t22, t11)),
        )
        for row, col, block in blocks:
            high, low = split(block)
            tmap[d, p, 0, row : row + TF, col : col + W] = high
            tmap[d, p, 1, row : row + TF, col : col + W] = low

    reach = (NZ // 2, NZ - 1 - NZ // 2)

    def t_copy(d, ring, k, zz, half):
        step = 1 if ring == 0 else -1
        rows = pl.ds(half * TF, TF)
        return pltpu.make_async_remote_copy(
            src_ref=tmsg.at[d, zz, rows, :],
            dst_ref=tmsg.at[d, zz, rows, :],
            send_sem=tsend.at[d, ring, k, half],
            recv_sem=trecv.at[d, ring, k, half],
            device_id=line_z(at_z(step)),
            device_id_type=MESH,
        )

    def t_begin(d):
        for half in range(2):
            for ring in range(2):
                if reach[ring] > 0:
                    t_copy(d, ring, 0, z, half).start()

    def t_step(d, k):
        for half in range(2):
            for ring in range(2):
                if k > reach[ring]:
                    continue
                source = at_z(-k if ring == 0 else k)
                t_copy(d, ring, k - 1, source, half).wait_recv()
                if k < reach[ring]:
                    t_copy(d, ring, k, source, half).start()
        for ring in range(2):
            if k <= reach[ring]:
                unpack(d, at_z(-k if ring == 0 else k))

    def t_end(d):
        for ring in range(2):
            for k in range(reach[ring]):
                for half in range(2):
                    t_copy(d, ring, k, at_z(-k if ring == 0 else k), half).wait_send()

    def multiply(left, right):
        high = jnp.concatenate([left[0, 0:TF, :], left[0, W : W + TF, :]], axis=0)
        low = jnp.concatenate([left[1, 0:TF, :], left[1, W : W + TF, :]], axis=0)
        return (
            jnp.dot(high, right[0], preferred_element_type=F32)
            + jnp.dot(high, right[1], preferred_element_type=F32)
            + jnp.dot(low, right[0], preferred_element_type=F32)
        )

    def keep(ref, value):
        for part, v in enumerate(split(value)):
            ref[part, 0:TF, :] = v[0:TF]
            ref[part, W : W + TF, :] = v[TF:]

    lane_d = lax.broadcasted_iota(jnp.int32, (2 * TF, W), 1)
    lane_q = lax.broadcasted_iota(jnp.int32, (TF // 2, W), 1)

    def d_copy(d, e, device):
        return pltpu.make_async_remote_copy(
            src_ref=dmsg.at[d],
            dst_ref=dbuf.at[d, e],
            send_sem=dsend.at[d, e],
            recv_sem=drecv.at[d, e],
            device_id=device,
            device_id_type=MESH,
        )

    def group_line(d, e):
        return ((x + e if d == 0 else x - e) * NZ + z, j)

    def map_levels(d):
        levels = [[tmap.at[d, p] for p in range(NZ)]]
        slot = 0
        while len(levels[-1]) > 2:
            count = len(levels[-1]) // 2
            levels.append([prod.at[d, slot + n] for n in range(count)])
            slot += count
        return levels

    def group_map(d):
        xp = x if d == 0 else NX - 1 - x
        levels = map_levels(d)
        for lower, upper in zip(levels, levels[1:]):
            for n, ref in enumerate(upper):
                keep(ref, multiply(lower[2 * n + 1], lower[2 * n]))
        total = multiply(levels[-1][1], levels[-1][0])
        rolled = pltpu.roll(total[:, W:], TF, 1)
        dmsg[d, 0 : 2 * TF, :] = jnp.where(lane_d < TF, total[:, :W], rolled)
        quarter = TF // 2
        rest = rolled[0:quarter]
        for q in range(1, 4):
            rest = jnp.where(
                lane_q < 32 * q, rest, pltpu.roll(rolled[q * quarter : (q + 1) * quarter], 32 * q, 1)
            )
        dmsg[d, 2 * TF :, :] = rest
        for e in range(1, NX - 1):

            @pl.when(jnp.logical_and(xp >= 1, xp + e <= NX - 1))
            def _():
                d_copy(d, e, group_line(d, e)).start()

    def group_arrive(d):
        xp = x if d == 0 else NX - 1 - x
        for source in range(1, NX - 1):

            @pl.when(xp > source)
            def _():
                e = xp - source
                d_copy(d, e, group_line(d, -e)).wait_recv()
                main = dbuf[d, e, 0 : 2 * TF, :]
                rest = dbuf[d, e, 2 * TF :, :]
                spread = jnp.concatenate(
                    [rest] + [pltpu.roll(rest, W - 32 * q, 1) for q in range(1, 4)], axis=0
                )
                zero = jnp.zeros((2 * TF, W), F32)
                left = jnp.where(lane_d < TF, main, zero)
                rolled = jnp.where(lane_d >= TF, main, jnp.where(lane_d < 32, spread, zero))
                right = pltpu.roll(rolled, 48, 1)
                keep(dmap.at[d, source - 1], jnp.concatenate([left, right], axis=1))

    def group_end(d):
        xp = x if d == 0 else NX - 1 - x
        for e in range(1, NX - 1):

            @pl.when(jnp.logical_and(xp >= 1, xp + e <= NX - 1))
            def _():
                d_copy(d, e, group_line(d, e)).wait_send()

    far_first = sorted(range(1, NZ), key=lambda d: (-min(d, NZ - d), d))

    def lanes_of(v):
        return lax.broadcasted_iota(jnp.int32, v.shape, 1)

    def pack(v0, v1):
        rolled = pltpu.roll(v1, TF, 1)
        half = CH // 2
        main = jnp.where(lanes_of(v0) < TF, v0, rolled)
        upper = rolled[:half]
        return main, jnp.where(lanes_of(upper) < 32, upper, pltpu.roll(rolled[half:], 32, 1))

    def unpacked(main, rest):
        lanes = lanes_of(main)
        zero = jnp.zeros(main.shape, F32)
        rolled = jnp.where(lanes >= TF, main, jnp.where(lanes < 32, rest, zero))
        return jnp.where(lanes < TF, main, zero), pltpu.roll(rolled, 48, 1)

    def unpack_piece(piece):
        rest = piece[CH:]
        rest = jnp.concatenate([rest, pltpu.roll(rest, 96, 1)], axis=0)
        return jnp.concatenate(unpacked(piece[:CH], rest), axis=1)

    def a_copy(h, d):
        zz = at_z(d)
        return pltpu.make_async_remote_copy(
            src_ref=sstage.at[h, zz],
            dst_ref=sbuf.at[h, z],
            send_sem=asend.at[h, d],
            recv_sem=arecv.at[h, d],
            device_id=line_z(zz),
            device_id_type=MESH,
        )

    def b_copy(h, d, p):
        return pltpu.make_async_remote_copy(
            src_ref=ostage.at[h, p],
            dst_ref=wbuf.at[h, z],
            send_sem=bsend.at[h, d],
            recv_sem=brecv.at[h, d],
            device_id=line_z(at_z(d)),
            device_id_type=MESH,
        )

    def g_copy(h, e, device):
        return pltpu.make_async_remote_copy(
            src_ref=gstage.at[h],
            dst_ref=gbuf.at[h, e],
            send_sem=gsend.at[h, e],
            recv_sem=grecv.at[h, e],
            device_id=device,
            device_id_type=MESH,
        )

    def p_copy(h, side, device):
        return pltpu.make_async_remote_copy(
            src_ref=pstage.at[h, side],
            dst_ref=pbuf.at[h, side],
            send_sem=psend.at[h, side],
            recv_sem=precv.at[h, side],
            device_id=device,
            device_id_type=MESH,
        )

    def solve(d, initial):
        first, second = (0, 1) if d == 0 else (1, 0)
        if initial:
            r1, r2 = base[first], base[second]
        else:
            r1, r2 = resid[first] - coupled(first, field[second]), resid[second]
        x1 = apply(invs[first], r1)
        x2 = apply(invs[second], r2 - coupled(second, x1))
        field[first] = x1
        field[second] = x2
        spar[first * W : first * W + W, :] = apply(tpad[d], x1)
        spar[second * W : second * W + W, :] = apply(tpad[d], x2)

    def send_line_traces(h, s):
        sa, sb = s[0:W], s[W:]
        s0 = jnp.where(a_is_0, sa, sb).T
        s1 = jnp.where(a_is_0, sb, sa).T
        for zz in range(NZ):
            rows = slice(zz * CH, (zz + 1) * CH)
            main, rest = pack(s0[rows], s1[rows])
            sstage[h, zz, 0:CH, :] = main
            sstage[h, zz, CH:, :] = rest
        for dist in far_first:
            a_copy(h, dist).start()
        sbuf[h, z] = sstage[h, z]

    def local_span_traces():
        for side, face in ((0, 3), (1, 2)):
            for pos in range(2):
                row = (2 * side + pos) * TF
                tloc[row : row + TF, :] = apply(trop_ref[face], field[pos])

    def at_start(k, d, action):
        if d == 0:
            pl.when(k == 0)(action)

    def finish(k, d):
        h = 2 * k + d
        first, second = (0, 1) if d == 0 else (1, 0)
        xp = x if d == 0 else NX - 1 - x
        at_start(k, d, lambda: group_map(0))
        for dist in far_first:
            a_copy(h, dist).wait_recv()

        for zz in range(NZ):
            p = zz if d == 0 else NZ - 1 - zz
            lsum[p] = unpack_piece(sbuf[h, zz])
        levels = map_levels(d)
        sums = [[lsum[p] for p in range(NZ)]]
        for maps in levels:
            low = sums[-1]
            sums.append([
                through(low[n], maps[n + 1][0], maps[n + 1][1]) + low[n + 1]
                for n in range(0, len(low), 2)
            ])
        v = sums[-1][0]
        gstage[h] = v
        for e in range(1, NX):

            @pl.when(xp + e <= NX - 1)
            def _():
                g_copy(h, e, group_line(d, e)).start()

        at_start(k, d, lambda: t_step(1, 1))
        pl.when(k == 0)(lambda: group_arrive(d))
        icur[...] = jnp.zeros((CH, 2 * W), F32)
        for source in range(NX - 1):

            @pl.when(xp > source)
            def _():
                e = xp - source
                g_copy(h, e, group_line(d, -e)).wait_recv()
                if source == 0:
                    icur[...] = gbuf[h, e]
                else:
                    icur[...] = gbuf[h, e] + through(
                        icur[...], dmap[d, source - 1, 0], dmap[d, source - 1, 1]
                    )

        flows = [icur[...]]
        for maps, low in zip(levels[::-1], sums[-2::-1]):
            wider = []
            for n, v in enumerate(flows):
                wider += [v, through(v, maps[2 * n][0], maps[2 * n][1]) + low[2 * n]]
            flows = wider
        for p in range(NZ):
            for part, v in zip((pl.ds(0, CH), pl.ds(CH, CH // 2)), pack(flows[p][:, :W], flows[p][:, W:])):
                ostage[h, p, part, :] = v
        for dist in far_first:
            zz = at_z(dist)
            b_copy(h, dist, zz if d == 0 else NZ - 1 - zz).start()
        own = z if d == 0 else NZ - 1 - z
        wbuf[h, z] = ostage[h, own]

        def more_maps():
            for n in range(2, NZ // 2):
                t_step(1, n)
            entry_map(0)

        at_start(k, d, more_maps)
        for dist in far_first:
            b_copy(h, dist, 0).wait_recv()

        main = jnp.concatenate([wbuf[h, zz, 0:CH, :] for zz in range(NZ)], axis=0)
        rest = jnp.concatenate([wbuf[h, zz, CH:, :] for zz in range(NZ)], axis=0)
        moved = pltpu.roll(rest, 96, 1)
        half = CH // 2
        rest = jnp.concatenate(
            [r[zz * half : (zz + 1) * half] for zz in range(NZ) for r in (rest, moved)], axis=0
        )
        w0, w1 = (w.T for w in unpacked(main, rest))
        wa = jnp.where(a_is_0, w0, w1)
        wb = jnp.where(a_is_0, w1, w0)
        sides = ((0, span_right), (1, span_left))

        def send_span_traces():
            t = tloc[...] - mapped(wmap.at[d], jnp.concatenate([wa, wb], axis=0))
            for side, device in sides:
                ta = t[2 * side * TF : (2 * side + 1) * TF]
                tb = t[(2 * side + 1) * TF : (2 * side + 2) * TF]
                pstage[h, side, 0] = jnp.where(a_is_0, ta, tb)
                pstage[h, side, 1] = jnp.where(a_is_0, tb, ta)
                p_copy(h, side, device).start()

        def prepare_next():
            for pos in range(2):
                resid[pos] = base[pos] - lifted[pos]
            solve(1 - d, False)

            def last_maps():
                if NZ // 2 > 1:
                    t_step(1, NZ // 2)
                t_end(1)
                group_end(0)

            at_start(k, d, last_maps)
            for side, device in sides:
                p_copy(h, side, device).wait_recv()
                t0 = pbuf[h, side, 0]
                t1 = pbuf[h, side, 1]
                row = 2 * side * W
                tfull[row : row + TF, :] = jnp.where(a_is_0, t0, t1)
                tfull[row + W : row + W + TF, :] = jnp.where(a_is_0, t1, t0)
            send_line_traces(h + 1, spar[...] + mapped(nmap.at[1 - d], tfull[...]))
            taken = [
                apply(lpad[2], tfull[pos * W : pos * W + W, :])
                + apply(lpad[3], tfull[(2 + pos) * W : (2 + pos) * W + W, :])
                for pos in range(2)
            ]
            z1 = apply(invs[second], taken[second])
            z2 = apply(invs[first], taken[first] - coupled(first, z1))
            field[second] = field[second] - z1
            field[first] = field[first] - z2
            local_span_traces()
            for side, device in sides:
                p_copy(h, side, device).wait_send()

        more = d == 0
        if more:
            send_span_traces()
        else:
            pl.when(k < SWEEPS - 1)(send_span_traces)
        lifted = (apply(lpad[d], wa), apply(lpad[d], wb))
        y1 = apply(invs[first], lifted[first])
        y2 = apply(invs[second], lifted[second] - coupled(second, y1))
        field[first] = field[first] - y1
        field[second] = field[second] - y2
        if more:
            prepare_next()
        else:
            pl.when(k < SWEEPS - 1)(prepare_next)

        for dist in far_first:
            a_copy(h, dist).wait_send()
            b_copy(h, dist, 0).wait_send()
        for e in range(1, NX):

            @pl.when(xp + e <= NX - 1)
            def _():
                g_copy(h, e, group_line(d, e)).wait_send()

    take_lift(0)
    take_coupling(1, b)
    own_map(0)
    pl.semaphore_wait(barrier, len(greeted))
    t_begin(0)
    for d in range(2):
        tpad[d, 0:TF, :] = trop_ref[1 - d]
    take_coupling(0, a)
    loads[-1].wait()
    base[0] = rhs_ref[a]
    base[1] = rhs_ref[b]
    solve(0, True)
    send_line_traces(0, spar[...])
    take_lift(1)
    own_map(1)
    unpack(0, z)
    chunks = [
        lambda: (span_map(0), unpack(1, z), local_span_traces()),
        lambda: (take_lift(2), take_lift(3), entry_map(1)),
        lambda: span_map(1),
    ]
    for k in range(1, NZ // 2 + 1):
        t_step(0, k)
        for chunk in chunks[:1] if k < NZ // 2 else chunks:
            chunk()
        chunks = chunks[1:]
    t_begin(1)
    t_end(0)

    def sweep(k, carry):
        finish(k, 0)

        @pl.when(k == 0)
        def _():
            group_map(1)

        finish(k, 1)
        return carry

    lax.fori_loop(0, SWEEPS, sweep, 0)
    group_end(1)
    out_ref[0] = jnp.where(a_is_0, field[0], field[1])
    out_ref[1] = jnp.where(a_is_0, field[1], field[0])


def solution(mesh):
    lines = mesh.shape["stream"]
    NZ = {32: 8, 8: 4, 4: 2}[lines]
    NX = lines // NZ
    NS = mesh.shape["span"]
    CH = W // NZ
    H = 2 * SWEEPS

    def local(rhs, inv_blocks, coupling, trace_ops, lift_ops, order, counts, neighbours, face_ids):
        dma = pltpu.SemaphoreType.DMA
        call = pl.pallas_call(
            functools.partial(kernel, NX, NZ, NS),
            out_shape=jax.ShapeDtypeStruct((2, B, W), F32),
            in_specs=[pl.BlockSpec(memory_space=pl.ANY)] * 9,
            out_specs=pl.BlockSpec(memory_space=pltpu.VMEM),
            scratch_shapes=[
                pltpu.SMEM((1, 1, 2), jnp.int32),
                pltpu.SMEM((1, 1), jnp.int32),
                pltpu.SMEM((1, 1, 2, 2), jnp.int32),
                pltpu.SMEM((1, 1, 2, 2), jnp.int32),
                pltpu.VMEM((2, B, W), F32),
                pltpu.VMEM((2, B, B), BF16),
                pltpu.VMEM((6, B, B), BF16),
                pltpu.VMEM((4, TF, B), BF16),
                pltpu.VMEM((4, TF, B), BF16),
                pltpu.VMEM((2, B, B), BF16),
                pltpu.VMEM((2, 2, B, B), BF16),
                pltpu.VMEM((4, B, W), BF16),
                pltpu.VMEM((4, W, B), BF16),
                pltpu.VMEM((2, W, B), BF16),
                pltpu.VMEM((2, B, W), F32),
                pltpu.VMEM((2, B, W), F32),
                pltpu.VMEM((2, B, W), F32),
                pltpu.VMEM((2, 3, B, W), F32),
                pltpu.VMEM((2, 2, 4 * TF, 2 * W), BF16),
                pltpu.VMEM((2, 2, 2 * W, 4 * W), BF16),
                pltpu.VMEM((4 * TF, W), F32),
                pltpu.VMEM((4 * W, W), F32),
                pltpu.VMEM((2 * W, W), F32),
                pltpu.VMEM((2, NZ, 2 * TF, W), F32),
                pltpu.VMEM((2, NZ, 2, 2 * W, 2 * W), BF16),
                pltpu.VMEM((2, max(NZ - 2, 1), 2, 2 * W, 2 * W), BF16),
                pltpu.VMEM((2, max(NX - 2, 1), 2, 2 * W, 2 * W), BF16),
                pltpu.VMEM((2, 5 * TF // 2, W), F32),
                pltpu.VMEM((2, NX, 5 * TF // 2, W), F32),
                pltpu.VMEM((H, NZ, 3 * CH // 2, W), F32),
                pltpu.VMEM((H, NZ, 3 * CH // 2, W), F32),
                pltpu.VMEM((NZ, CH, 2 * W), F32),
                pltpu.VMEM((H, NZ, 3 * CH // 2, W), F32),
                pltpu.VMEM((H, NZ, 3 * CH // 2, W), F32),
                pltpu.VMEM((H, CH, 2 * W), F32),
                pltpu.VMEM((H, NX, CH, 2 * W), F32),
                pltpu.VMEM((CH, 2 * W), F32),
                pltpu.VMEM((H, 2, 2, TF, W), F32),
                pltpu.VMEM((H, 2, 2, TF, W), F32),
                dma((9,)),
                dma((2, 2, NZ, 2)), dma((2, 2, NZ, 2)),
                dma((H, NZ)), dma((H, NZ)),
                dma((H, NZ)), dma((H, NZ)),
                dma((H, NX)), dma((H, NX)),
                dma((2, NX)), dma((2, NX)),
                dma((H, 2)), dma((H, 2)),
            ],
            compiler_params=pltpu.CompilerParams(
                collective_id=0, has_side_effects=True, vmem_limit_bytes=60 << 20
            ),
        )
        result = call(
            order, counts, neighbours, face_ids,
            rhs[0, 0], inv_blocks[0, 0], coupling, trace_ops, lift_ops.transpose(0, 2, 1),
        )
        return result[None, None]

    placed = (
        P("stream", "span", None, None, None),
        P("stream", "span", None, None, None),
        P(),
        P(),
        P(),
        P("stream", "span", None),
        P("stream", "span"),
        P("stream", "span", None, None),
        P("stream", "span", None, None),
    )
    return jax.shard_map(
        local,
        mesh=mesh,
        in_specs=placed,
        out_specs=P("stream", "span", None, None, None),
        check_vma=False,
    )
```

```python
import functools

import jax
import jax.numpy as jnp
from jax import lax
from jax.experimental import pallas as pl
from jax.experimental.pallas import tpu as pltpu
from jax.sharding import PartitionSpec as P

MESH = pl.DeviceIdType.MESH
F32 = jnp.float32
BF16 = jnp.bfloat16
SWEEPS = 2
B = 320
TF = 80
W = 128


def split(v):
    high = v.astype(BF16)
    return high, (v - high.astype(F32)).astype(BF16)


def apply(operator, v):
    high, low = split(v)
    both = jnp.dot(operator, jnp.concatenate([high, low], axis=1), preferred_element_type=F32)
    return both[:, :W] + both[:, W:]


def nt(a, b):
    return lax.dot_general(a, b, (((1,), (1,)), ((), ())), preferred_element_type=F32)


def through(v, high_map, low_map):
    high, low = split(v)
    rows = v.shape[0]
    both = nt(jnp.concatenate([high, low], axis=0), high_map)
    return both[:rows] + both[rows:] + nt(high, low_map)


def kernel(
    NX, NZ, NS,
    order_hbm, count_hbm, nbr_hbm, fid_hbm, rhs_hbm, inv_hbm, coup_hbm, trop_hbm, liftt_hbm,
    out_ref,
    order_ref, count_ref, nbr_ref, fid_ref, rhs_ref, inv_ref, coup_ref, trop_ref, liftt_ref,
    invs, coups, lpad, ltpad, tpad, base, resid, field,
    kept, rmap, wmap, nmap, tloc, tfull, spar,
    tmsg, tmap, prod, dmap, dmsg, dbuf, sstage, sbuf, lsum, ostage, wbuf, gstage, gbuf, icur, pstage, pbuf,
    insem, tsend, trecv, asend, arecv, bsend, brecv, gsend, grecv, dsend, drecv, psend, precv,
):
    CH = W // NZ
    i = lax.axis_index("stream")
    j = lax.axis_index("span")
    z = lax.rem(i, NZ)
    x = lax.div(i, NZ)

    def at_z(offset):
        return lax.rem(z + (offset + NZ), NZ)

    def line_z(zz):
        return (x * NZ + zz, j)

    span_left = (i, lax.rem(j + NS - 1, NS))
    span_right = (i, lax.rem(j + 1, NS))

    barrier = pltpu.get_barrier_semaphore()
    greeted = [line_z(at_z(d)) for d in range(1, NZ)] + [span_left, span_right]
    greeted += [(lax.rem(x + e, NX) * NZ + z, j) for e in range(1, NX)]
    for device in greeted:
        pl.semaphore_signal(barrier, inc=1, device_id=device, device_id_type=MESH)

    pairs = (
        (order_hbm, order_ref), (count_hbm, count_ref), (nbr_hbm, nbr_ref), (fid_hbm, fid_ref),
        (inv_hbm, inv_ref), (coup_hbm, coup_ref), (liftt_hbm, liftt_ref), (trop_hbm, trop_ref),
        (rhs_hbm, rhs_ref),
    )
    loads = [pltpu.make_async_copy(src, dst, insem.at[n]) for n, (src, dst) in enumerate(pairs)]
    for load in loads:
        load.start()

    tmap[:, :, :, TF:W, :] = jnp.zeros((2, NZ, 2, W - TF, 2 * W), BF16)
    tmap[:, :, :, W + TF :, :] = jnp.zeros((2, NZ, 2, W - TF, 2 * W), BF16)
    tfull[...] = jnp.zeros(tfull.shape, F32)
    for ref in (wmap, nmap):
        ref[...] = jnp.zeros(ref.shape, BF16)
    gap = W - TF
    for d in range(2):
        for rows in (pl.ds(TF, gap), pl.ds(W + TF, gap)):
            prod[d, :, :, rows, :] = jnp.zeros((prod.shape[1], 2, gap, 2 * W), BF16)
            dmap[d, :, :, rows, :] = jnp.zeros((dmap.shape[1], 2, gap, 2 * W), BF16)
    ltpad[...] = jnp.zeros(ltpad.shape, BF16)
    tpad[...] = jnp.zeros(tpad.shape, BF16)
    row = lax.broadcasted_iota(jnp.int32, (B, B), 0)
    col = lax.broadcasted_iota(jnp.int32, (B, B), 1)
    identity = jnp.where(row == col, 1.0, 0.0).astype(BF16)
    for load in loads[:-1]:
        load.wait()

    a = order_ref[0, 0, 0]
    b = order_ref[0, 0, 1]
    a_is_0 = a == 0
    live = count_ref[0, 0] > 1
    zero_block = jnp.zeros((B, B), BF16)
    invs[0] = inv_ref[a]
    invs[1] = jnp.where(live, inv_ref[b], zero_block)

    def take_lift(q):
        ltpad[q, 0:TF, :] = liftt_ref[q]
        lpad[q] = nt(identity, ltpad[q]).astype(BF16)

    def take_coupling(pos, slot):
        for m in range(2):
            present = nbr_ref[0, 0, slot, m] < 2
            coups[pos, m] = jnp.where(present, coup_ref[fid_ref[0, 0, slot, m]], zero_block)

    def coupled(pos, v):
        high, low = split(v)
        v2 = jnp.concatenate([high, low], axis=1)
        both = jnp.dot(coups[pos, 0], v2, preferred_element_type=F32) + jnp.dot(
            coups[pos, 1], v2, preferred_element_type=F32
        )
        return both[:, :W] + both[:, W:]

    lane = lax.broadcasted_iota(jnp.int32, (TF, W), 1)

    def response(d, q):
        first, second = (0, 1) if d == 0 else (1, 0)
        u1 = jnp.dot(invs[first], lpad[q], preferred_element_type=F32)
        u2 = jnp.dot(invs[second], lpad[q], preferred_element_type=F32)
        v = apply(invs[second], coupled(second, u1))
        return u1, u2, v

    def own_map(d):
        u1, u2, v = response(d, d)
        for n, part in enumerate((u1, u2, v)):
            kept[d, n] = part
        trace = trop_ref[1 - d]
        t11 = -apply(trace, u1)
        t22 = -apply(trace, u2)
        t21 = apply(trace, v)
        first_is_0 = jnp.where(a_is_0, 1.0 - d, 0.0 + d).astype(F32)
        flag = jnp.zeros((TF, W), F32) + first_is_0
        upper = jnp.where(lane < TF, t11, jnp.where(lane < 112, pltpu.roll(t22, 32, 1), flag))
        lower = jnp.where(lane < TF, t21, pltpu.roll(t22, TF, 1))
        tmsg[d, z, 0:TF, :] = upper
        tmsg[d, z, TF : 2 * TF, :] = lower

    def put(ref, row, col, value):
        for part, v in enumerate(split(value)):
            ref[part, row : row + value.shape[0], col : col + W] = v

    def mapped(ref, v):
        high, low = split(v)
        both = jnp.concatenate([high, low], axis=1)
        y = jnp.dot(ref[0], both, preferred_element_type=F32)
        y = y[:, :W] + y[:, W:]
        return y + jnp.dot(ref[1], high, preferred_element_type=F32)

    def span_map(d):
        first, second = (0, 1) if d == 0 else (1, 0)
        put(rmap.at[d], first * B, first * W, kept[d, 0])
        put(rmap.at[d], first * B, second * W, jnp.zeros((B, W), F32))
        put(rmap.at[d], second * B, second * W, kept[d, 1])
        put(rmap.at[d], second * B, first * W, -kept[d, 2])
        for side, face in ((0, 3), (1, 2)):
            trace = trop_ref[face]
            rows = (2 * side + first) * TF, (2 * side + second) * TF
            put(wmap.at[d], rows[0], first * W, apply(trace, kept[d, 0]))
            put(wmap.at[d], rows[1], second * W, apply(trace, kept[d, 1]))
            put(wmap.at[d], rows[1], first * W, -apply(trace, kept[d, 2]))

    def entry_map(d):
        first, second = (0, 1) if d == 0 else (1, 0)
        for side in range(2):
            u1, u2, v = response(d, 2 + side)
            col = 2 * side * W
            put(nmap.at[d], first * W, col + first * W, -apply(tpad[d], u1))
            put(nmap.at[d], second * W, col + second * W, -apply(tpad[d], u2))
            put(nmap.at[d], second * W, col + first * W, apply(tpad[d], v))

    def unpack(d, zz):
        p = zz if d == 0 else NZ - 1 - zz
        upper = tmsg[d, zz, 0:TF, :]
        lower = tmsg[d, zz, TF : 2 * TF, :]
        flag = jnp.sum(jnp.where(lane == 120, upper, 0.0), axis=1, keepdims=True) > 0.5
        zero = jnp.zeros((TF, W), F32)
        t11 = jnp.where(lane < TF, upper, zero)
        t21 = jnp.where(lane < TF, lower, zero)
        t22 = jnp.where(
            lane < 48,
            pltpu.roll(lower, 48, 1),
            jnp.where(lane < TF, pltpu.roll(upper, 96, 1), zero),
        )
        blocks = (
            (0, 0, jnp.where(flag, t11, t22)),
            (0, W, jnp.where(flag, zero, t21)),
            (W, 0, jnp.where(flag, t21, zero)),
            (W, W, jnp.where(flag, t22, t11)),
        )
        for row, col, block in blocks:
            high, low = split(block)
            tmap[d, p, 0, row : row + TF, col : col + W] = high
            tmap[d, p, 1, row : row + TF, col : col + W] = low

    reach = (NZ // 2, NZ - 1 - NZ // 2)

    def t_copy(d, ring, k, zz, half):
        step = 1 if ring == 0 else -1
        rows = pl.ds(half * TF, TF)
        return pltpu.make_async_remote_copy(
            src_ref=tmsg.at[d, zz, rows, :],
            dst_ref=tmsg.at[d, zz, rows, :],
            send_sem=tsend.at[d, ring, k, half],
            recv_sem=trecv.at[d, ring, k, half],
            device_id=line_z(at_z(step)),
            device_id_type=MESH,
        )

    def t_begin(d):
        for half in range(2):
            for ring in range(2):
                if reach[ring] > 0:
                    t_copy(d, ring, 0, z, half).start()

    def t_step(d, k):
        for half in range(2):
            for ring in range(2):
                if k > reach[ring]:
                    continue
                source = at_z(-k if ring == 0 else k)
                t_copy(d, ring, k - 1, source, half).wait_recv()
                if k < reach[ring]:
                    t_copy(d, ring, k, source, half).start()
        for ring in range(2):
            if k <= reach[ring]:
                unpack(d, at_z(-k if ring == 0 else k))

    def t_end(d):
        for ring in range(2):
            for k in range(reach[ring]):
                for half in range(2):
                    t_copy(d, ring, k, at_z(-k if ring == 0 else k), half).wait_send()

    def multiply(left, right):
        high = jnp.concatenate([left[0, 0:TF, :], left[0, W : W + TF, :]], axis=0)
        low = jnp.concatenate([left[1, 0:TF, :], left[1, W : W + TF, :]], axis=0)
        return (
            jnp.dot(high, right[0], preferred_element_type=F32)
            + jnp.dot(high, right[1], preferred_element_type=F32)
            + jnp.dot(low, right[0], preferred_element_type=F32)
        )

    def keep(ref, value):
        for part, v in enumerate(split(value)):
            ref[part, 0:TF, :] = v[0:TF]
            ref[part, W : W + TF, :] = v[TF:]

    lane_d = lax.broadcasted_iota(jnp.int32, (2 * TF, W), 1)
    lane_q = lax.broadcasted_iota(jnp.int32, (TF // 2, W), 1)

    def d_copy(d, e, device):
        return pltpu.make_async_remote_copy(
            src_ref=dmsg.at[d],
            dst_ref=dbuf.at[d, e],
            send_sem=dsend.at[d, e],
            recv_sem=drecv.at[d, e],
            device_id=device,
            device_id_type=MESH,
        )

    def group_line(d, e):
        return ((x + e if d == 0 else x - e) * NZ + z, j)

    def map_levels(d):
        levels = [[tmap.at[d, p] for p in range(NZ)]]
        slot = 0
        while len(levels[-1]) > 2:
            count = len(levels[-1]) // 2
            levels.append([prod.at[d, slot + n] for n in range(count)])
            slot += count
        return levels

    def group_map(d):
        xp = x if d == 0 else NX - 1 - x
        levels = map_levels(d)
        for lower, upper in zip(levels, levels[1:]):
            for n, ref in enumerate(upper):
                keep(ref, multiply(lower[2 * n + 1], lower[2 * n]))
        total = multiply(levels[-1][1], levels[-1][0])
        rolled = pltpu.roll(total[:, W:], TF, 1)
        dmsg[d, 0 : 2 * TF, :] = jnp.where(lane_d < TF, total[:, :W], rolled)
        quarter = TF // 2
        rest = rolled[0:quarter]
        for q in range(1, 4):
            rest = jnp.where(
                lane_q < 32 * q, rest, pltpu.roll(rolled[q * quarter : (q + 1) * quarter], 32 * q, 1)
            )
        dmsg[d, 2 * TF :, :] = rest
        for e in range(1, NX - 1):

            @pl.when(jnp.logical_and(xp >= 1, xp + e <= NX - 1))
            def _():
                d_copy(d, e, group_line(d, e)).start()

    def group_arrive(d):
        xp = x if d == 0 else NX - 1 - x
        for source in range(1, NX - 1):

            @pl.when(xp > source)
            def _():
                e = xp - source
                d_copy(d, e, group_line(d, -e)).wait_recv()
                main = dbuf[d, e, 0 : 2 * TF, :]
                rest = dbuf[d, e, 2 * TF :, :]
                spread = jnp.concatenate(
                    [rest] + [pltpu.roll(rest, W - 32 * q, 1) for q in range(1, 4)], axis=0
                )
                zero = jnp.zeros((2 * TF, W), F32)
                left = jnp.where(lane_d < TF, main, zero)
                rolled = jnp.where(lane_d >= TF, main, jnp.where(lane_d < 32, spread, zero))
                right = pltpu.roll(rolled, 48, 1)
                keep(dmap.at[d, source - 1], jnp.concatenate([left, right], axis=1))

    def group_end(d):
        xp = x if d == 0 else NX - 1 - x
        for e in range(1, NX - 1):

            @pl.when(jnp.logical_and(xp >= 1, xp + e <= NX - 1))
            def _():
                d_copy(d, e, group_line(d, e)).wait_send()

    far_first = sorted(range(1, NZ), key=lambda d: (-min(d, NZ - d), d))

    def lanes_of(v):
        return lax.broadcasted_iota(jnp.int32, v.shape, 1)

    def pack(v0, v1):
        rolled = pltpu.roll(v1, TF, 1)
        half = CH // 2
        main = jnp.where(lanes_of(v0) < TF, v0, rolled)
        upper = rolled[:half]
        return main, jnp.where(lanes_of(upper) < 32, upper, pltpu.roll(rolled[half:], 32, 1))

    def unpacked(main, rest):
        lanes = lanes_of(main)
        zero = jnp.zeros(main.shape, F32)
        rolled = jnp.where(lanes >= TF, main, jnp.where(lanes < 32, rest, zero))
        return jnp.where(lanes < TF, main, zero), pltpu.roll(rolled, 48, 1)

    def unpack_piece(piece):
        rest = piece[CH:]
        rest = jnp.concatenate([rest, pltpu.roll(rest, 96, 1)], axis=0)
        return jnp.concatenate(unpacked(piece[:CH], rest), axis=1)

    def a_copy(h, d):
        zz = at_z(d)
        return pltpu.make_async_remote_copy(
            src_ref=sstage.at[h, zz],
            dst_ref=sbuf.at[h, z],
            send_sem=asend.at[h, d],
            recv_sem=arecv.at[h, d],
            device_id=line_z(zz),
            device_id_type=MESH,
        )

    def b_copy(h, d, p):
        return pltpu.make_async_remote_copy(
            src_ref=ostage.at[h, p],
            dst_ref=wbuf.at[h, z],
            send_sem=bsend.at[h, d],
            recv_sem=brecv.at[h, d],
            device_id=line_z(at_z(d)),
            device_id_type=MESH,
        )

    def g_copy(h, e, device):
        return pltpu.make_async_remote_copy(
            src_ref=gstage.at[h],
            dst_ref=gbuf.at[h, e],
            send_sem=gsend.at[h, e],
            recv_sem=grecv.at[h, e],
            device_id=device,
            device_id_type=MESH,
        )

    def p_copy(h, side, device):
        return pltpu.make_async_remote_copy(
            src_ref=pstage.at[h, side],
            dst_ref=pbuf.at[h, side],
            send_sem=psend.at[h, side],
            recv_sem=precv.at[h, side],
            device_id=device,
            device_id_type=MESH,
        )

    def solve(d, initial):
        first, second = (0, 1) if d == 0 else (1, 0)
        if initial:
            r1, r2 = base[first], base[second]
        else:
            r1, r2 = resid[first] - coupled(first, field[second]), resid[second]
        x1 = apply(invs[first], r1)
        x2 = apply(invs[second], r2 - coupled(second, x1))
        field[first] = x1
        field[second] = x2
        spar[first * W : first * W + W, :] = apply(tpad[d], x1)
        spar[second * W : second * W + W, :] = apply(tpad[d], x2)

    def send_line_traces(h, s):
        sa, sb = s[0:W], s[W:]
        s0 = jnp.where(a_is_0, sa, sb).T
        s1 = jnp.where(a_is_0, sb, sa).T
        for zz in range(NZ):
            rows = slice(zz * CH, (zz + 1) * CH)
            main, rest = pack(s0[rows], s1[rows])
            sstage[h, zz, 0:CH, :] = main
            sstage[h, zz, CH:, :] = rest
        for dist in far_first:
            a_copy(h, dist).start()
        sbuf[h, z] = sstage[h, z]

    def local_span_traces():
        for side, face in ((0, 3), (1, 2)):
            for pos in range(2):
                row = (2 * side + pos) * TF
                tloc[row : row + TF, :] = apply(trop_ref[face], field[pos])

    def at_start(k, d, action):
        if d == 0:
            pl.when(k == 0)(action)

    def finish(k, d):
        h = 2 * k + d
        first, second = (0, 1) if d == 0 else (1, 0)
        xp = x if d == 0 else NX - 1 - x
        at_start(k, d, lambda: group_map(0))
        for dist in far_first:
            a_copy(h, dist).wait_recv()

        for zz in range(NZ):
            p = zz if d == 0 else NZ - 1 - zz
            lsum[p] = unpack_piece(sbuf[h, zz])
        levels = map_levels(d)
        sums = [[lsum[p] for p in range(NZ)]]
        for maps in levels:
            low = sums[-1]
            sums.append([
                through(low[n], maps[n + 1][0], maps[n + 1][1]) + low[n + 1]
                for n in range(0, len(low), 2)
            ])
        v = sums[-1][0]
        gstage[h] = v
        for e in range(1, NX):

            @pl.when(xp + e <= NX - 1)
            def _():
                g_copy(h, e, group_line(d, e)).start()

        at_start(k, d, lambda: t_step(1, 1))
        pl.when(k == 0)(lambda: group_arrive(d))
        icur[...] = jnp.zeros((CH, 2 * W), F32)
        for source in range(NX - 1):

            @pl.when(xp > source)
            def _():
                e = xp - source
                g_copy(h, e, group_line(d, -e)).wait_recv()
                if source == 0:
                    icur[...] = gbuf[h, e]
                else:
                    icur[...] = gbuf[h, e] + through(
                        icur[...], dmap[d, source - 1, 0], dmap[d, source - 1, 1]
                    )

        flows = [icur[...]]
        for maps, low in zip(levels[::-1], sums[-2::-1]):
            wider = []
            for n, v in enumerate(flows):
                wider += [v, through(v, maps[2 * n][0], maps[2 * n][1]) + low[2 * n]]
            flows = wider
        for p in range(NZ):
            for part, v in zip((pl.ds(0, CH), pl.ds(CH, CH // 2)), pack(flows[p][:, :W], flows[p][:, W:])):
                ostage[h, p, part, :] = v
        for dist in far_first:
            zz = at_z(dist)
            b_copy(h, dist, zz if d == 0 else NZ - 1 - zz).start()
        own = z if d == 0 else NZ - 1 - z
        wbuf[h, z] = ostage[h, own]

        def more_maps():
            for n in range(2, NZ // 2):
                t_step(1, n)
            entry_map(0)

        at_start(k, d, more_maps)
        for dist in far_first:
            b_copy(h, dist, 0).wait_recv()

        main = jnp.concatenate([wbuf[h, zz, 0:CH, :] for zz in range(NZ)], axis=0)
        rest = jnp.concatenate([wbuf[h, zz, CH:, :] for zz in range(NZ)], axis=0)
        moved = pltpu.roll(rest, 96, 1)
        half = CH // 2
        rest = jnp.concatenate(
            [r[zz * half : (zz + 1) * half] for zz in range(NZ) for r in (rest, moved)], axis=0
        )
        w0, w1 = (w.T for w in unpacked(main, rest))
        wa = jnp.where(a_is_0, w0, w1)
        wb = jnp.where(a_is_0, w1, w0)
        sides = ((0, span_right), (1, span_left))
        inflow = jnp.concatenate([wa, wb], axis=0)

        def send_span_traces():
            t = tloc[...] - mapped(wmap.at[d], inflow)
            for side, device in sides:
                ta = t[2 * side * TF : (2 * side + 1) * TF]
                tb = t[(2 * side + 1) * TF : (2 * side + 2) * TF]
                pstage[h, side, 0] = jnp.where(a_is_0, ta, tb)
                pstage[h, side, 1] = jnp.where(a_is_0, tb, ta)
                p_copy(h, side, device).start()

        def prepare_next():
            resid[0] = base[0] - apply(lpad[d], wa)
            resid[1] = base[1] - apply(lpad[d], wb)
            solve(1 - d, False)

            def last_maps():
                if NZ // 2 > 1:
                    t_step(1, NZ // 2)
                t_end(1)
                group_end(0)

            at_start(k, d, last_maps)
            for side, device in sides:
                p_copy(h, side, device).wait_recv()
                t0 = pbuf[h, side, 0]
                t1 = pbuf[h, side, 1]
                row = 2 * side * W
                tfull[row : row + TF, :] = jnp.where(a_is_0, t0, t1)
                tfull[row + W : row + W + TF, :] = jnp.where(a_is_0, t1, t0)
            send_line_traces(h + 1, spar[...] + mapped(nmap.at[1 - d], tfull[...]))
            taken = [
                apply(lpad[2], tfull[pos * W : pos * W + W, :])
                + apply(lpad[3], tfull[(2 + pos) * W : (2 + pos) * W + W, :])
                for pos in range(2)
            ]
            z1 = apply(invs[second], taken[second])
            z2 = apply(invs[first], taken[first] - coupled(first, z1))
            field[second] = field[second] - z1
            field[first] = field[first] - z2
            local_span_traces()
            for side, device in sides:
                p_copy(h, side, device).wait_send()

        more = d == 0
        if more:
            send_span_traces()
        else:
            pl.when(k < SWEEPS - 1)(send_span_traces)
        taken = mapped(rmap.at[d], inflow)
        field[0] = field[0] - taken[0:B]
        field[1] = field[1] - taken[B:]
        if more:
            prepare_next()
        else:
            pl.when(k < SWEEPS - 1)(prepare_next)

        for dist in far_first:
            a_copy(h, dist).wait_send()
            b_copy(h, dist, 0).wait_send()
        for e in range(1, NX):

            @pl.when(xp + e <= NX - 1)
            def _():
                g_copy(h, e, group_line(d, e)).wait_send()

    take_lift(0)
    take_coupling(1, b)
    own_map(0)
    pl.semaphore_wait(barrier, len(greeted))
    t_begin(0)
    for d in range(2):
        tpad[d, 0:TF, :] = trop_ref[1 - d]
    take_coupling(0, a)
    loads[-1].wait()
    base[0] = rhs_ref[a]
    base[1] = rhs_ref[b]
    solve(0, True)
    take_lift(1)
    own_map(1)
    unpack(0, z)
    chunks = [
        lambda: (span_map(0), unpack(1, z), local_span_traces()),
        lambda: (take_lift(2), take_lift(3), entry_map(1)),
        lambda: span_map(1),
    ]
    for k in range(1, NZ // 2 + 1):
        t_step(0, k)
        if k == max(NZ // 2 - 2, 1):
            send_line_traces(0, spar[...])
        for chunk in chunks[:1] if k < NZ // 2 else chunks:
            chunk()
        chunks = chunks[1:]
    t_begin(1)
    t_end(0)

    def sweep(k, carry):
        finish(k, 0)

        @pl.when(k == 0)
        def _():
            group_map(1)

        finish(k, 1)
        return carry

    lax.fori_loop(0, SWEEPS, sweep, 0)
    group_end(1)
    out_ref[0] = jnp.where(a_is_0, field[0], field[1])
    out_ref[1] = jnp.where(a_is_0, field[1], field[0])


def solution(mesh):
    lines = mesh.shape["stream"]
    NZ = {32: 8, 8: 4, 4: 2}[lines]
    NX = lines // NZ
    NS = mesh.shape["span"]
    CH = W // NZ
    H = 2 * SWEEPS

    def local(rhs, inv_blocks, coupling, trace_ops, lift_ops, order, counts, neighbours, face_ids):
        dma = pltpu.SemaphoreType.DMA
        call = pl.pallas_call(
            functools.partial(kernel, NX, NZ, NS),
            out_shape=pltpu.VMEM((2, B, W), F32),
            in_specs=[pl.BlockSpec(memory_space=pl.ANY)] * 9,
            out_specs=pl.BlockSpec(memory_space=pltpu.VMEM),
            scratch_shapes=[
                pltpu.SMEM((1, 1, 2), jnp.int32),
                pltpu.SMEM((1, 1), jnp.int32),
                pltpu.SMEM((1, 1, 2, 2), jnp.int32),
                pltpu.SMEM((1, 1, 2, 2), jnp.int32),
                pltpu.VMEM((2, B, W), F32),
                pltpu.VMEM((2, B, B), BF16),
                pltpu.VMEM((6, B, B), BF16),
                pltpu.VMEM((4, TF, B), BF16),
                pltpu.VMEM((4, TF, B), BF16),
                pltpu.VMEM((2, B, B), BF16),
                pltpu.VMEM((2, 2, B, B), BF16),
                pltpu.VMEM((4, B, W), BF16),
                pltpu.VMEM((4, W, B), BF16),
                pltpu.VMEM((2, W, B), BF16),
                pltpu.VMEM((2, B, W), F32),
                pltpu.VMEM((2, B, W), F32),
                pltpu.VMEM((2, B, W), F32),
                pltpu.VMEM((2, 3, B, W), F32),
                pltpu.VMEM((2, 2, 2 * B, 2 * W), BF16),
                pltpu.VMEM((2, 2, 4 * TF, 2 * W), BF16),
                pltpu.VMEM((2, 2, 2 * W, 4 * W), BF16),
                pltpu.VMEM((4 * TF, W), F32),
                pltpu.VMEM((4 * W, W), F32),
                pltpu.VMEM((2 * W, W), F32),
                pltpu.VMEM((2, NZ, 2 * TF, W), F32),
                pltpu.VMEM((2, NZ, 2, 2 * W, 2 * W), BF16),
                pltpu.VMEM((2, max(NZ - 2, 1), 2, 2 * W, 2 * W), BF16),
                pltpu.VMEM((2, max(NX - 2, 1), 2, 2 * W, 2 * W), BF16),
                pltpu.VMEM((2, 5 * TF // 2, W), F32),
                pltpu.VMEM((2, NX, 5 * TF // 2, W), F32),
                pltpu.VMEM((H, NZ, 3 * CH // 2, W), F32),
                pltpu.VMEM((H, NZ, 3 * CH // 2, W), F32),
                pltpu.VMEM((NZ, CH, 2 * W), F32),
                pltpu.VMEM((H, NZ, 3 * CH // 2, W), F32),
                pltpu.VMEM((H, NZ, 3 * CH // 2, W), F32),
                pltpu.VMEM((H, CH, 2 * W), F32),
                pltpu.VMEM((H, NX, CH, 2 * W), F32),
                pltpu.VMEM((CH, 2 * W), F32),
                pltpu.VMEM((H, 2, 2, TF, W), F32),
                pltpu.VMEM((H, 2, 2, TF, W), F32),
                dma((9,)),
                dma((2, 2, NZ, 2)), dma((2, 2, NZ, 2)),
                dma((H, NZ)), dma((H, NZ)),
                dma((H, NZ)), dma((H, NZ)),
                dma((H, NX)), dma((H, NX)),
                dma((2, NX)), dma((2, NX)),
                dma((H, 2)), dma((H, 2)),
            ],
            compiler_params=pltpu.CompilerParams(
                collective_id=0, has_side_effects=True, vmem_limit_bytes=60 << 20
            ),
        )
        result = call(
            order, counts, neighbours, face_ids,
            rhs[0, 0], inv_blocks[0, 0], coupling, trace_ops, lift_ops.transpose(0, 2, 1),
        )
        return result[None, None]

    placed = (
        P("stream", "span", None, None, None),
        P("stream", "span", None, None, None),
        P(),
        P(),
        P(),
        P("stream", "span", None),
        P("stream", "span"),
        P("stream", "span", None, None),
        P("stream", "span", None, None),
    )
    return jax.shard_map(
        local,
        mesh=mesh,
        in_specs=placed,
        out_specs=P("stream", "span", None, None, None),
        check_vma=False,
    )
```

```python
import functools

import jax
import jax.numpy as jnp
from jax import lax
from jax.experimental import pallas as pl
from jax.experimental.pallas import tpu as pltpu
from jax.sharding import PartitionSpec as P

MESH = pl.DeviceIdType.MESH
F32 = jnp.float32
BF16 = jnp.bfloat16
SWEEPS = 2
B = 320
TF = 80
W = 128


def split(v):
    high = v.astype(BF16)
    return high, (v - high.astype(F32)).astype(BF16)


def apply(operator, v):
    high, low = split(v)
    both = jnp.dot(operator, jnp.concatenate([high, low], axis=1), preferred_element_type=F32)
    return both[:, :W] + both[:, W:]


def nt(a, b):
    return lax.dot_general(a, b, (((1,), (1,)), ((), ())), preferred_element_type=F32)


def through(v, high_map, low_map):
    high, low = split(v)
    rows = v.shape[0]
    both = nt(jnp.concatenate([high, low], axis=0), high_map)
    return both[:rows] + both[rows:] + nt(high, low_map)


def kernel(
    NX, NZ, NS,
    order_hbm, count_hbm, nbr_hbm, fid_hbm, rhs_hbm, inv_hbm, coup_hbm, trop_hbm, liftt_hbm,
    out_ref,
    order_ref, count_ref, nbr_ref, fid_ref, rhs_ref, inv_ref, coup_ref, trop_ref, liftt_ref,
    invs, coups, lpad, ltpad, tpad, base, resid, field,
    kept, rmap, wmap, nmap, tloc, tfull, spar,
    tmsg, tmap, prod, dmap, dmsg, dbuf, sstage, sbuf, lsum, ostage, wbuf, gstage, gbuf, icur, pstage, pbuf,
    insem, tsend, trecv, asend, arecv, bsend, brecv, gsend, grecv, dsend, drecv, psend, precv,
):
    CH = W // NZ
    i = lax.axis_index("stream")
    j = lax.axis_index("span")
    z = lax.rem(i, NZ)
    x = lax.div(i, NZ)

    def at_z(offset):
        return lax.rem(z + (offset + NZ), NZ)

    def line_z(zz):
        return (x * NZ + zz, j)

    span_left = (i, lax.rem(j + NS - 1, NS))
    span_right = (i, lax.rem(j + 1, NS))

    barrier = pltpu.get_barrier_semaphore()
    greeted = [line_z(at_z(d)) for d in range(1, NZ)] + [span_left, span_right]
    greeted += [(lax.rem(x + e, NX) * NZ + z, j) for e in range(1, NX)]
    for device in greeted:
        pl.semaphore_signal(barrier, inc=1, device_id=device, device_id_type=MESH)

    pairs = (
        (order_hbm, order_ref), (count_hbm, count_ref), (nbr_hbm, nbr_ref), (fid_hbm, fid_ref),
        (inv_hbm, inv_ref), (coup_hbm, coup_ref), (liftt_hbm, liftt_ref), (trop_hbm, trop_ref),
        (rhs_hbm, rhs_ref),
    )
    loads = [pltpu.make_async_copy(src, dst, insem.at[n]) for n, (src, dst) in enumerate(pairs)]
    for load in loads:
        load.start()

    tmap[:, :, :, TF:W, :] = jnp.zeros((2, NZ, 2, W - TF, 2 * W), BF16)
    tmap[:, :, :, W + TF :, :] = jnp.zeros((2, NZ, 2, W - TF, 2 * W), BF16)
    tfull[...] = jnp.zeros(tfull.shape, F32)
    for ref in (wmap, nmap):
        ref[...] = jnp.zeros(ref.shape, BF16)
    gap = W - TF
    for d in range(2):
        for rows in (pl.ds(TF, gap), pl.ds(W + TF, gap)):
            prod[d, :, :, rows, :] = jnp.zeros((prod.shape[1], 2, gap, 2 * W), BF16)
            dmap[d, :, :, rows, :] = jnp.zeros((dmap.shape[1], 2, gap, 2 * W), BF16)
    ltpad[...] = jnp.zeros(ltpad.shape, BF16)
    tpad[...] = jnp.zeros(tpad.shape, BF16)
    row = lax.broadcasted_iota(jnp.int32, (B, B), 0)
    col = lax.broadcasted_iota(jnp.int32, (B, B), 1)
    identity = jnp.where(row == col, 1.0, 0.0).astype(BF16)
    for load in loads[:-1]:
        load.wait()

    a = order_ref[0, 0, 0]
    b = order_ref[0, 0, 1]
    a_is_0 = a == 0
    live = count_ref[0, 0] > 1
    zero_block = jnp.zeros((B, B), BF16)
    invs[0] = inv_ref[a]
    invs[1] = jnp.where(live, inv_ref[b], zero_block)

    def take_lift(q):
        ltpad[q, 0:TF, :] = liftt_ref[q]
        lpad[q] = nt(identity, ltpad[q]).astype(BF16)

    def take_coupling(pos, slot):
        for m in range(2):
            present = nbr_ref[0, 0, slot, m] < 2
            coups[pos, m] = jnp.where(present, coup_ref[fid_ref[0, 0, slot, m]], zero_block)

    def coupled(pos, v):
        high, low = split(v)
        v2 = jnp.concatenate([high, low], axis=1)
        both = jnp.dot(coups[pos, 0], v2, preferred_element_type=F32) + jnp.dot(
            coups[pos, 1], v2, preferred_element_type=F32
        )
        return both[:, :W] + both[:, W:]

    lane = lax.broadcasted_iota(jnp.int32, (TF, W), 1)

    def response(d, q):
        first, second = (0, 1) if d == 0 else (1, 0)
        u1 = jnp.dot(invs[first], lpad[q], preferred_element_type=F32)
        u2 = jnp.dot(invs[second], lpad[q], preferred_element_type=F32)
        v = apply(invs[second], coupled(second, u1))
        return u1, u2, v

    def own_map(d):
        u1, u2, v = response(d, d)
        for n, part in enumerate((u1, u2, v)):
            kept[d, n] = part
        trace = trop_ref[1 - d]
        t11 = -apply(trace, u1)
        t22 = -apply(trace, u2)
        t21 = apply(trace, v)
        first_is_0 = jnp.where(a_is_0, 1.0 - d, 0.0 + d).astype(F32)
        flag = jnp.zeros((TF, W), F32) + first_is_0
        upper = jnp.where(lane < TF, t11, jnp.where(lane < 112, pltpu.roll(t22, 32, 1), flag))
        lower = jnp.where(lane < TF, t21, pltpu.roll(t22, TF, 1))
        tmsg[d, z, 0:TF, :] = upper
        tmsg[d, z, TF : 2 * TF, :] = lower

    def put(ref, row, col, value):
        for part, v in enumerate(split(value)):
            ref[part, row : row + value.shape[0], col : col + W] = v

    def mapped(ref, v):
        high, low = split(v)
        both = jnp.concatenate([high, low], axis=1)
        y = jnp.dot(ref[0], both, preferred_element_type=F32)
        y = y[:, :W] + y[:, W:]
        return y + jnp.dot(ref[1], high, preferred_element_type=F32)

    def span_map(d):
        first, second = (0, 1) if d == 0 else (1, 0)
        put(rmap.at[d], first * B, first * W, kept[d, 0])
        put(rmap.at[d], first * B, second * W, jnp.zeros((B, W), F32))
        put(rmap.at[d], second * B, second * W, kept[d, 1])
        put(rmap.at[d], second * B, first * W, -kept[d, 2])
        for side, face in ((0, 3), (1, 2)):
            trace = trop_ref[face]
            rows = (2 * side + first) * TF, (2 * side + second) * TF
            put(wmap.at[d], rows[0], first * W, apply(trace, kept[d, 0]))
            put(wmap.at[d], rows[1], second * W, apply(trace, kept[d, 1]))
            put(wmap.at[d], rows[1], first * W, -apply(trace, kept[d, 2]))

    def entry_map(d):
        first, second = (0, 1) if d == 0 else (1, 0)
        for side in range(2):
            u1, u2, v = response(d, 2 + side)
            col = 2 * side * W
            put(nmap.at[d], first * W, col + first * W, -apply(tpad[d], u1))
            put(nmap.at[d], second * W, col + second * W, -apply(tpad[d], u2))
            put(nmap.at[d], second * W, col + first * W, apply(tpad[d], v))

    def unpack(d, zz):
        p = zz if d == 0 else NZ - 1 - zz
        upper = tmsg[d, zz, 0:TF, :]
        lower = tmsg[d, zz, TF : 2 * TF, :]
        flag = jnp.sum(jnp.where(lane == 120, upper, 0.0), axis=1, keepdims=True) > 0.5
        zero = jnp.zeros((TF, W), F32)
        t11 = jnp.where(lane < TF, upper, zero)
        t21 = jnp.where(lane < TF, lower, zero)
        t22 = jnp.where(
            lane < 48,
            pltpu.roll(lower, 48, 1),
            jnp.where(lane < TF, pltpu.roll(upper, 96, 1), zero),
        )
        blocks = (
            (0, 0, jnp.where(flag, t11, t22)),
            (0, W, jnp.where(flag, zero, t21)),
            (W, 0, jnp.where(flag, t21, zero)),
            (W, W, jnp.where(flag, t22, t11)),
        )
        for row, col, block in blocks:
            high, low = split(block)
            tmap[d, p, 0, row : row + TF, col : col + W] = high
            tmap[d, p, 1, row : row + TF, col : col + W] = low

    reach = (NZ // 2, NZ - 1 - NZ // 2)

    def t_copy(d, ring, k, zz, quarter):
        step = 1 if ring == 0 else -1
        rows = pl.ds(quarter * (TF // 2), TF // 2)
        return pltpu.make_async_remote_copy(
            src_ref=tmsg.at[d, zz, rows, :],
            dst_ref=tmsg.at[d, zz, rows, :],
            send_sem=tsend.at[d, ring, k, quarter],
            recv_sem=trecv.at[d, ring, k, quarter],
            device_id=line_z(at_z(step)),
            device_id_type=MESH,
        )

    def t_begin(d):
        for quarter in range(4):
            for ring in range(2):
                if reach[ring] > 0:
                    t_copy(d, ring, 0, z, quarter).start()

    def t_step(d, k):
        for quarter in range(4):
            for ring in range(2):
                if k > reach[ring]:
                    continue
                source = at_z(-k if ring == 0 else k)
                t_copy(d, ring, k - 1, source, quarter).wait_recv()
                if k < reach[ring]:
                    t_copy(d, ring, k, source, quarter).start()
        for ring in range(2):
            if k <= reach[ring]:
                unpack(d, at_z(-k if ring == 0 else k))

    def t_end(d):
        for ring in range(2):
            for k in range(reach[ring]):
                for quarter in range(4):
                    t_copy(d, ring, k, at_z(-k if ring == 0 else k), quarter).wait_send()

    def multiply(left, right):
        high = jnp.concatenate([left[0, 0:TF, :], left[0, W : W + TF, :]], axis=0)
        low = jnp.concatenate([left[1, 0:TF, :], left[1, W : W + TF, :]], axis=0)
        return (
            jnp.dot(high, right[0], preferred_element_type=F32)
            + jnp.dot(high, right[1], preferred_element_type=F32)
            + jnp.dot(low, right[0], preferred_element_type=F32)
        )

    def keep(ref, value):
        for part, v in enumerate(split(value)):
            ref[part, 0:TF, :] = v[0:TF]
            ref[part, W : W + TF, :] = v[TF:]

    lane_d = lax.broadcasted_iota(jnp.int32, (2 * TF, W), 1)
    lane_q = lax.broadcasted_iota(jnp.int32, (TF // 2, W), 1)

    def d_copy(d, e, device):
        return pltpu.make_async_remote_copy(
            src_ref=dmsg.at[d],
            dst_ref=dbuf.at[d, e],
            send_sem=dsend.at[d, e],
            recv_sem=drecv.at[d, e],
            device_id=device,
            device_id_type=MESH,
        )

    def group_line(d, e):
        return ((x + e if d == 0 else x - e) * NZ + z, j)

    def map_levels(d):
        levels = [[tmap.at[d, p] for p in range(NZ)]]
        slot = 0
        while len(levels[-1]) > 2:
            count = len(levels[-1]) // 2
            levels.append([prod.at[d, slot + n] for n in range(count)])
            slot += count
        return levels

    def group_map(d):
        xp = x if d == 0 else NX - 1 - x
        levels = map_levels(d)
        for lower, upper in zip(levels, levels[1:]):
            for n, ref in enumerate(upper):
                keep(ref, multiply(lower[2 * n + 1], lower[2 * n]))
        total = multiply(levels[-1][1], levels[-1][0])
        rolled = pltpu.roll(total[:, W:], TF, 1)
        dmsg[d, 0 : 2 * TF, :] = jnp.where(lane_d < TF, total[:, :W], rolled)
        quarter = TF // 2
        rest = rolled[0:quarter]
        for q in range(1, 4):
            rest = jnp.where(
                lane_q < 32 * q, rest, pltpu.roll(rolled[q * quarter : (q + 1) * quarter], 32 * q, 1)
            )
        dmsg[d, 2 * TF :, :] = rest
        for e in range(1, NX - 1):

            @pl.when(jnp.logical_and(xp >= 1, xp + e <= NX - 1))
            def _():
                d_copy(d, e, group_line(d, e)).start()

    def group_arrive(d):
        xp = x if d == 0 else NX - 1 - x
        for source in range(1, NX - 1):

            @pl.when(xp > source)
            def _():
                e = xp - source
                d_copy(d, e, group_line(d, -e)).wait_recv()
                main = dbuf[d, e, 0 : 2 * TF, :]
                rest = dbuf[d, e, 2 * TF :, :]
                spread = jnp.concatenate(
                    [rest] + [pltpu.roll(rest, W - 32 * q, 1) for q in range(1, 4)], axis=0
                )
                zero = jnp.zeros((2 * TF, W), F32)
                left = jnp.where(lane_d < TF, main, zero)
                rolled = jnp.where(lane_d >= TF, main, jnp.where(lane_d < 32, spread, zero))
                right = pltpu.roll(rolled, 48, 1)
                keep(dmap.at[d, source - 1], jnp.concatenate([left, right], axis=1))

    def group_end(d):
        xp = x if d == 0 else NX - 1 - x
        for e in range(1, NX - 1):

            @pl.when(jnp.logical_and(xp >= 1, xp + e <= NX - 1))
            def _():
                d_copy(d, e, group_line(d, e)).wait_send()

    far_first = sorted(range(1, NZ), key=lambda d: (-min(d, NZ - d), d))

    def lanes_of(v):
        return lax.broadcasted_iota(jnp.int32, v.shape, 1)

    def pack(v0, v1):
        rolled = pltpu.roll(v1, TF, 1)
        half = CH // 2
        main = jnp.where(lanes_of(v0) < TF, v0, rolled)
        upper = rolled[:half]
        return main, jnp.where(lanes_of(upper) < 32, upper, pltpu.roll(rolled[half:], 32, 1))

    def unpacked(main, rest):
        lanes = lanes_of(main)
        zero = jnp.zeros(main.shape, F32)
        rolled = jnp.where(lanes >= TF, main, jnp.where(lanes < 32, rest, zero))
        return jnp.where(lanes < TF, main, zero), pltpu.roll(rolled, 48, 1)

    def unpack_piece(piece):
        rest = piece[CH:]
        rest = jnp.concatenate([rest, pltpu.roll(rest, 96, 1)], axis=0)
        return jnp.concatenate(unpacked(piece[:CH], rest), axis=1)

    def a_copy(h, d):
        zz = at_z(d)
        return pltpu.make_async_remote_copy(
            src_ref=sstage.at[h, zz],
            dst_ref=sbuf.at[h, z],
            send_sem=asend.at[h, d],
            recv_sem=arecv.at[h, d],
            device_id=line_z(zz),
            device_id_type=MESH,
        )

    def b_copy(h, d, p):
        return pltpu.make_async_remote_copy(
            src_ref=ostage.at[h, p],
            dst_ref=wbuf.at[h, z],
            send_sem=bsend.at[h, d],
            recv_sem=brecv.at[h, d],
            device_id=line_z(at_z(d)),
            device_id_type=MESH,
        )

    def g_copy(h, e, device):
        return pltpu.make_async_remote_copy(
            src_ref=gstage.at[h],
            dst_ref=gbuf.at[h, e],
            send_sem=gsend.at[h, e],
            recv_sem=grecv.at[h, e],
            device_id=device,
            device_id_type=MESH,
        )

    def p_copy(h, side, device):
        return pltpu.make_async_remote_copy(
            src_ref=pstage.at[h, side],
            dst_ref=pbuf.at[h, side],
            send_sem=psend.at[h, side],
            recv_sem=precv.at[h, side],
            device_id=device,
            device_id_type=MESH,
        )

    def solve(d, initial):
        first, second = (0, 1) if d == 0 else (1, 0)
        if initial:
            r1, r2 = base[first], base[second]
        else:
            r1, r2 = resid[first] - coupled(first, field[second]), resid[second]
        x1 = apply(invs[first], r1)
        x2 = apply(invs[second], r2 - coupled(second, x1))
        field[first] = x1
        field[second] = x2
        spar[first * W : first * W + W, :] = apply(tpad[d], x1)
        spar[second * W : second * W + W, :] = apply(tpad[d], x2)

    def send_line_traces(h, s):
        sa, sb = s[0:W], s[W:]
        s0 = jnp.where(a_is_0, sa, sb).T
        s1 = jnp.where(a_is_0, sb, sa).T
        for zz in range(NZ):
            rows = slice(zz * CH, (zz + 1) * CH)
            main, rest = pack(s0[rows], s1[rows])
            sstage[h, zz, 0:CH, :] = main
            sstage[h, zz, CH:, :] = rest
        for dist in far_first:
            a_copy(h, dist).start()
        sbuf[h, z] = sstage[h, z]

    def local_span_traces():
        for side, face in ((0, 3), (1, 2)):
            for pos in range(2):
                row = (2 * side + pos) * TF
                tloc[row : row + TF, :] = apply(trop_ref[face], field[pos])

    def at_start(k, d, action):
        if d == 0:
            pl.when(k == 0)(action)

    def finish(k, d):
        h = 2 * k + d
        first, second = (0, 1) if d == 0 else (1, 0)
        xp = x if d == 0 else NX - 1 - x
        at_start(k, d, lambda: group_map(0))
        for dist in far_first:
            a_copy(h, dist).wait_recv()

        for zz in range(NZ):
            p = zz if d == 0 else NZ - 1 - zz
            lsum[p] = unpack_piece(sbuf[h, zz])
        levels = map_levels(d)
        sums = [[lsum[p] for p in range(NZ)]]
        for maps in levels:
            low = sums[-1]
            sums.append([
                through(low[n], maps[n + 1][0], maps[n + 1][1]) + low[n + 1]
                for n in range(0, len(low), 2)
            ])
        v = sums[-1][0]
        gstage[h] = v
        for e in range(1, NX):

            @pl.when(xp + e <= NX - 1)
            def _():
                g_copy(h, e, group_line(d, e)).start()

        at_start(k, d, lambda: t_step(1, 1))
        pl.when(k == 0)(lambda: group_arrive(d))
        icur[...] = jnp.zeros((CH, 2 * W), F32)
        for source in range(NX - 1):

            @pl.when(xp > source)
            def _():
                e = xp - source
                g_copy(h, e, group_line(d, -e)).wait_recv()
                if source == 0:
                    icur[...] = gbuf[h, e]
                else:
                    icur[...] = gbuf[h, e] + through(
                        icur[...], dmap[d, source - 1, 0], dmap[d, source - 1, 1]
                    )

        flows = [icur[...]]
        for maps, low in zip(levels[::-1], sums[-2::-1]):
            wider = []
            for n, v in enumerate(flows):
                wider += [v, through(v, maps[2 * n][0], maps[2 * n][1]) + low[2 * n]]
            flows = wider
        for p in range(NZ):
            for part, v in zip((pl.ds(0, CH), pl.ds(CH, CH // 2)), pack(flows[p][:, :W], flows[p][:, W:])):
                ostage[h, p, part, :] = v
        for dist in far_first:
            zz = at_z(dist)
            b_copy(h, dist, zz if d == 0 else NZ - 1 - zz).start()
        own = z if d == 0 else NZ - 1 - z
        wbuf[h, z] = ostage[h, own]

        def more_maps():
            for n in range(2, NZ // 2):
                t_step(1, n)
            entry_map(0)

        at_start(k, d, more_maps)
        for dist in far_first:
            b_copy(h, dist, 0).wait_recv()

        main = jnp.concatenate([wbuf[h, zz, 0:CH, :] for zz in range(NZ)], axis=0)
        rest = jnp.concatenate([wbuf[h, zz, CH:, :] for zz in range(NZ)], axis=0)
        moved = pltpu.roll(rest, 96, 1)
        half = CH // 2
        rest = jnp.concatenate(
            [r[zz * half : (zz + 1) * half] for zz in range(NZ) for r in (rest, moved)], axis=0
        )
        w0, w1 = (w.T for w in unpacked(main, rest))
        wa = jnp.where(a_is_0, w0, w1)
        wb = jnp.where(a_is_0, w1, w0)
        sides = ((0, span_right), (1, span_left))
        inflow = jnp.concatenate([wa, wb], axis=0)

        def send_span_traces():
            t = tloc[...] - mapped(wmap.at[d], inflow)
            for side, device in sides:
                ta = t[2 * side * TF : (2 * side + 1) * TF]
                tb = t[(2 * side + 1) * TF : (2 * side + 2) * TF]
                pstage[h, side, 0] = jnp.where(a_is_0, ta, tb)
                pstage[h, side, 1] = jnp.where(a_is_0, tb, ta)
                p_copy(h, side, device).start()

        def prepare_next():
            resid[0] = base[0] - apply(lpad[d], wa)
            resid[1] = base[1] - apply(lpad[d], wb)
            solve(1 - d, False)

            def last_maps():
                if NZ // 2 > 1:
                    t_step(1, NZ // 2)
                t_end(1)
                group_end(0)

            at_start(k, d, last_maps)
            for side, device in sides:
                p_copy(h, side, device).wait_recv()
                t0 = pbuf[h, side, 0]
                t1 = pbuf[h, side, 1]
                row = 2 * side * W
                tfull[row : row + TF, :] = jnp.where(a_is_0, t0, t1)
                tfull[row + W : row + W + TF, :] = jnp.where(a_is_0, t1, t0)
            send_line_traces(h + 1, spar[...] + mapped(nmap.at[1 - d], tfull[...]))
            taken = [
                apply(lpad[2], tfull[pos * W : pos * W + W, :])
                + apply(lpad[3], tfull[(2 + pos) * W : (2 + pos) * W + W, :])
                for pos in range(2)
            ]
            z1 = apply(invs[second], taken[second])
            z2 = apply(invs[first], taken[first] - coupled(first, z1))
            field[second] = field[second] - z1
            field[first] = field[first] - z2
            local_span_traces()
            for side, device in sides:
                p_copy(h, side, device).wait_send()

        more = d == 0
        if more:
            send_span_traces()
        else:
            pl.when(k < SWEEPS - 1)(send_span_traces)
        taken = mapped(rmap.at[d], inflow)
        field[0] = field[0] - taken[0:B]
        field[1] = field[1] - taken[B:]
        if more:
            prepare_next()
        else:
            pl.when(k < SWEEPS - 1)(prepare_next)

        for dist in far_first:
            a_copy(h, dist).wait_send()
            b_copy(h, dist, 0).wait_send()
        for e in range(1, NX):

            @pl.when(xp + e <= NX - 1)
            def _():
                g_copy(h, e, group_line(d, e)).wait_send()

    take_lift(0)
    take_coupling(1, b)
    own_map(0)
    pl.semaphore_wait(barrier, len(greeted))
    t_begin(0)
    for d in range(2):
        tpad[d, 0:TF, :] = trop_ref[1 - d]
    take_coupling(0, a)
    loads[-1].wait()
    base[0] = rhs_ref[a]
    base[1] = rhs_ref[b]
    solve(0, True)
    take_lift(1)
    own_map(1)
    unpack(0, z)
    chunks = [
        lambda: (span_map(0), unpack(1, z), local_span_traces()),
        lambda: (take_lift(2), take_lift(3), entry_map(1)),
        lambda: span_map(1),
    ]
    for k in range(1, NZ // 2 + 1):
        t_step(0, k)
        if k == max(NZ // 2 - 2, 1):
            send_line_traces(0, spar[...])
        for chunk in chunks[:1] if k < NZ // 2 else chunks:
            chunk()
        chunks = chunks[1:]
    t_begin(1)
    t_end(0)

    def sweep(k, carry):
        finish(k, 0)

        @pl.when(k == 0)
        def _():
            group_map(1)

        finish(k, 1)
        return carry

    lax.fori_loop(0, SWEEPS, sweep, 0)
    group_end(1)
    out_ref[0] = jnp.where(a_is_0, field[0], field[1])
    out_ref[1] = jnp.where(a_is_0, field[1], field[0])


def solution(mesh):
    lines = mesh.shape["stream"]
    NZ = {32: 8, 8: 4, 4: 2}[lines]
    NX = lines // NZ
    NS = mesh.shape["span"]
    CH = W // NZ
    H = 2 * SWEEPS

    def local(rhs, inv_blocks, coupling, trace_ops, lift_ops, order, counts, neighbours, face_ids):
        dma = pltpu.SemaphoreType.DMA
        call = pl.pallas_call(
            functools.partial(kernel, NX, NZ, NS),
            out_shape=pltpu.VMEM((2, B, W), F32),
            in_specs=[pl.BlockSpec(memory_space=pl.ANY)] * 9,
            out_specs=pl.BlockSpec(memory_space=pltpu.VMEM),
            scratch_shapes=[
                pltpu.SMEM((1, 1, 2), jnp.int32),
                pltpu.SMEM((1, 1), jnp.int32),
                pltpu.SMEM((1, 1, 2, 2), jnp.int32),
                pltpu.SMEM((1, 1, 2, 2), jnp.int32),
                pltpu.VMEM((2, B, W), F32),
                pltpu.VMEM((2, B, B), BF16),
                pltpu.VMEM((6, B, B), BF16),
                pltpu.VMEM((4, TF, B), BF16),
                pltpu.VMEM((4, TF, B), BF16),
                pltpu.VMEM((2, B, B), BF16),
                pltpu.VMEM((2, 2, B, B), BF16),
                pltpu.VMEM((4, B, W), BF16),
                pltpu.VMEM((4, W, B), BF16),
                pltpu.VMEM((2, W, B), BF16),
                pltpu.VMEM((2, B, W), F32),
                pltpu.VMEM((2, B, W), F32),
                pltpu.VMEM((2, B, W), F32),
                pltpu.VMEM((2, 3, B, W), F32),
                pltpu.VMEM((2, 2, 2 * B, 2 * W), BF16),
                pltpu.VMEM((2, 2, 4 * TF, 2 * W), BF16),
                pltpu.VMEM((2, 2, 2 * W, 4 * W), BF16),
                pltpu.VMEM((4 * TF, W), F32),
                pltpu.VMEM((4 * W, W), F32),
                pltpu.VMEM((2 * W, W), F32),
                pltpu.VMEM((2, NZ, 2 * TF, W), F32),
                pltpu.VMEM((2, NZ, 2, 2 * W, 2 * W), BF16),
                pltpu.VMEM((2, max(NZ - 2, 1), 2, 2 * W, 2 * W), BF16),
                pltpu.VMEM((2, max(NX - 2, 1), 2, 2 * W, 2 * W), BF16),
                pltpu.VMEM((2, 5 * TF // 2, W), F32),
                pltpu.VMEM((2, NX, 5 * TF // 2, W), F32),
                pltpu.VMEM((H, NZ, 3 * CH // 2, W), F32),
                pltpu.VMEM((H, NZ, 3 * CH // 2, W), F32),
                pltpu.VMEM((NZ, CH, 2 * W), F32),
                pltpu.VMEM((H, NZ, 3 * CH // 2, W), F32),
                pltpu.VMEM((H, NZ, 3 * CH // 2, W), F32),
                pltpu.VMEM((H, CH, 2 * W), F32),
                pltpu.VMEM((H, NX, CH, 2 * W), F32),
                pltpu.VMEM((CH, 2 * W), F32),
                pltpu.VMEM((H, 2, 2, TF, W), F32),
                pltpu.VMEM((H, 2, 2, TF, W), F32),
                dma((9,)),
                dma((2, 2, NZ, 4)), dma((2, 2, NZ, 4)),
                dma((H, NZ)), dma((H, NZ)),
                dma((H, NZ)), dma((H, NZ)),
                dma((H, NX)), dma((H, NX)),
                dma((2, NX)), dma((2, NX)),
                dma((H, 2)), dma((H, 2)),
            ],
            compiler_params=pltpu.CompilerParams(
                collective_id=0, has_side_effects=True, vmem_limit_bytes=60 << 20
            ),
        )
        result = call(
            order, counts, neighbours, face_ids,
            rhs[0, 0], inv_blocks[0, 0], coupling, trace_ops, lift_ops.transpose(0, 2, 1),
        )
        return result[None, None]

    placed = (
        P("stream", "span", None, None, None),
        P("stream", "span", None, None, None),
        P(),
        P(),
        P(),
        P("stream", "span", None),
        P("stream", "span"),
        P("stream", "span", None, None),
        P("stream", "span", None, None),
    )
    return jax.shard_map(
        local,
        mesh=mesh,
        in_specs=placed,
        out_specs=P("stream", "span", None, None, None),
        check_vma=False,
    )
```
